128 devices in a mesh: seq: 32 (over x, z_lo, y), tp: 4 (over z_hi, core).
Axes of the slice: x: 4, y: 4, z: 4 (z_hi: 2, z_lo: 2; z = z_hi * 2 + z_lo), core: 2. Of those that a mesh axis runs over, the one named last changes fastest.
Arguments:
- x_codes: int32 [4096, 8192], P('seq', 'tp'), may hold values from -127 to 127
- w_codes: int32 [3, 8192, 8192], P(None, 'tp', 'seq'), may hold values from -127 to 127
- req_mult: int32 [3, 8192], P(None, 'seq'), may hold values from 64 to 255
- req_shift: int32 [3, 8192], P(None, 'seq'), may hold values from 20 to 21
- short_codes: int32 [3, 3, 8192], P(None, None, 'seq'), may hold values from -127 to 127
- residue_codes: int32 [16, 8192], P(None, 'seq'), may hold values from -127 to 127
- rates: float32 [16, 8192], P(None, 'seq'), may hold values from 0.00024414062 to 0.0625
- skip_gain: float32 [8192], P('seq'), may hold values from -4 to 4
Outputs:
- gated: bfloat16 [4096, 8192], P(('seq', 'tp'))
The draws below stay inside these ranges and needn't reach their ends.
All inputs are finite; a program needn't handle non-finite values.
Results may differ from the reference program's by a relative error of at most 0.0057.
Values may be sent and summed in bfloat16 or wider, within the bound.
A program may use at most 256 MiB of HBM per device.

```python
import math
import jax
import jax.numpy as jnp
from jax import lax

D = 8192
STATES = 16
SHORT = 3
SEQLEN = 4096


def plant(values, key, smallest, top_value):
    place = [jax.random.randint(jax.random.fold_in(key, axis), (), 0, length) for axis, length in enumerate(values.shape)]
    widest = values.shape.index(max(values.shape))
    next_to = place[:widest] + [(place[widest] + 1) % values.shape[widest]] + place[widest + 1:]
    return values.at[tuple(place)].set(smallest).at[tuple(next_to)].set(top_value)


def block_scale(own_key, shape, split, low, top_value):
    def one(position, blocks):
        heights = jax.random.uniform(jax.random.fold_in(jax.random.fold_in(own_key, 6), position), (blocks,), jnp.float32, low / len(split), top_value / len(split))
        return jnp.repeat(jnp.exp(heights), shape[position] // blocks).reshape((-1,) + (1,) * (len(shape) - position - 1))

    gain = one(*split[0])
    for cut in split[1:]:
        gain = gain * one(*cut)
    return gain


def scatter_about(rng, shape, scale, most, pieces=(), kind=jnp.bfloat16):
    values = scale * jax.random.normal(rng, shape, jnp.float32)
    if pieces:
        values = values * block_scale(rng, shape, pieces, -0.22, 0.18)
    return jnp.clip(values, -most, most).astype(kind)


def setup_inputs(seed: int = 0) -> dict:
    streams_of = jax.random.split(jax.random.key(seed), 9)
    x_codes = plant(jax.random.randint(streams_of[0], (SEQLEN, D), -127, 128), jax.random.fold_in(streams_of[0], 1), -127, 127).astype(jnp.int32)
    w_codes = plant(jax.random.randint(streams_of[1], (3, D, D), -127, 128), jax.random.fold_in(streams_of[1], 1), -127, 127).astype(jnp.int32)
    req_mult = plant(jax.random.randint(streams_of[2], (3, D), 64, 256), jax.random.fold_in(streams_of[2], 1), 64, 255).astype(jnp.int32)
    req_shift = plant(jax.random.randint(streams_of[3], (3, D), 20, 22), jax.random.fold_in(streams_of[3], 1), 20, 21).astype(jnp.int32)
    short_codes = plant(jax.random.randint(streams_of[4], (SHORT, 3, D), -127, 128), jax.random.fold_in(streams_of[4], 1), -127, 127).astype(jnp.int32)
    residue_codes = plant(jax.random.randint(streams_of[5], (STATES, D), -127, 128), jax.random.fold_in(streams_of[5], 1), -127, 127).astype(jnp.int32)
    rates = jnp.clip(jnp.exp(math.log(0.0625) - 5.5451774 * jax.random.uniform(streams_of[6], (STATES, D), jnp.float32) ** block_scale(streams_of[6], (STATES, D), ((1, 32),), -0.2, 0.2)), 0.00024414062, 0.0625)
    skip_gain = scatter_about(streams_of[7], (D,), 1.0, 4.0, ((0, 32),), jnp.float32)
    return dict(x_codes=x_codes, w_codes=w_codes, req_mult=req_mult, req_shift=req_shift, short_codes=short_codes, residue_codes=residue_codes, rates=rates, skip_gain=skip_gain)


def shifted_lag(values, lag):
    if lag == 0:
        return values
    padded = jnp.pad(values, ((0, 0), (0, 0), (lag, 0)))
    return padded[:, :, :values.shape[2]]

def reference(x_codes, w_codes, req_mult, req_shift, short_codes, residue_codes, rates, skip_gain):
    seqlen = x_codes.shape[0]
    x_float = x_codes.astype(jnp.float32)
    requant = req_mult.astype(jnp.float32) * jnp.exp2(-req_shift.astype(jnp.float32))
    coded_list = []
    for which in range(3):
        summed = jnp.dot(x_float, w_codes[which].astype(jnp.float32), precision=lax.Precision.HIGHEST)
        coded_list.append(jnp.clip(summed * requant[which][None, :], -127.0, 127.0).astype(jnp.bfloat16))
    coded = jnp.stack(coded_list)
    values = jnp.transpose(coded.astype(jnp.float32), (0, 2, 1)) * (1.0 / 64.0)
    short_taps = short_codes.astype(jnp.float32) * (1.0 / 128.0)
    featured = short_taps[0][:, :, None] * shifted_lag(values, 0)
    for lag in range(1, SHORT):
        featured = featured + short_taps[lag][:, :, None] * shifted_lag(values, lag)
    queries = featured[0]
    drive = featured[1] * featured[2]
    coeffs = residue_codes.astype(jnp.float32) * (1.0 / (127.0 * math.sqrt(STATES))) * jnp.sqrt(-jnp.expm1(-2.0 * rates))
    positions = jnp.arange(seqlen).astype(jnp.float32)
    kernel = jnp.zeros(drive.shape, jnp.float32)
    for mode in range(STATES):
        kernel = kernel + coeffs[mode][:, None] * jnp.exp(-rates[mode][:, None] * positions[None, :])
    length_fft = 2 * seqlen
    spectrum = jnp.fft.rfft(drive, length_fft, axis=1) * jnp.fft.rfft(kernel, length_fft, axis=1)
    convolved = jnp.fft.irfft(spectrum, length_fft, axis=1)[:, :seqlen]
    mixed = convolved + skip_gain[:, None] * drive
    gated = (queries * mixed).astype(jnp.bfloat16)
    return jnp.transpose(gated)
```

```python
import functools
import math

import jax
import jax.numpy as jnp
from jax import lax
from jax.experimental import pallas as pl
from jax.experimental.pallas import tpu as pltpu
from jax.sharding import PartitionSpec as P

MESH = pl.DeviceIdType.MESH
F32 = jnp.float32
BF16 = jnp.bfloat16
LANES = 128
CHUNKS = 8
RING = 4
GROUPS = 5


def halves_of(which, array):
    return jnp.where(which == 0, array[..., :LANES], array[..., LANES:])


def small_expm1_neg(z):
    poly = jnp.ones_like(z)
    for order in range(8, 1, -1):
        poly = 1.0 - (z * (1.0 / order)) * poly
    return z * poly


def hyena_kernel(
    x_ref, w_hbm, mult_ref, shift_ref, short_ref, residue_ref, rates_ref, skip_ref,
    out_ref,
    own_x, all_x, raw_w, both_w, sums, far_sums, coded, tails, sib_tails, ends, sib_ends,
    starts, queries, drives, gated, staged,
    first_send, first_recv, raw_sem, w_send, w_recv, ring_send, ring_recv,
    far_send, far_recv, tail_send, tail_recv, end_send, end_recv, out_send, out_recv,
):
    seq = lax.axis_index("seq")
    tp = lax.axis_index("tp")
    devices = 128
    y = lax.rem(seq, 4)
    layer = lax.rem(seq // 4, 2)
    x = seq // 8
    core = lax.rem(tp, 2)
    high = tp // 2
    rows, feats = own_x.shape
    half_rows = rows // 2
    modes = residue_ref.shape[0]
    step_count = coded.shape[1] // CHUNKS

    def device(x_at, y_at, layer_at, high_at, core_at):
        return ((x_at * 2 + layer_at) * 4 + y_at, high_at * 2 + core_at)

    def wrap(value):
        return lax.rem(value + 2 * RING, RING)

    barrier = pltpu.get_barrier_semaphore()
    me = seq * 4 + tp

    @pl.loop(1, devices)
    def _(offset):
        other = lax.rem(me + offset, devices)
        pl.semaphore_signal(
            barrier, inc=1, device_id=(other // 4, lax.rem(other, 4)), device_id_type=MESH
        )

    w_chunks = raw_w.shape[0]
    w_rows = raw_w.shape[2]
    for chunk in range(w_chunks):
        pltpu.make_async_copy(
            w_hbm.at[:, pl.ds(chunk * w_rows, w_rows), :], raw_w.at[chunk], raw_sem.at[chunk]
        ).start()
    own_x[...] = x_ref[...].astype(F32).astype(BF16)

    def convert_chunk(chunk):
        pltpu.make_async_copy(
            w_hbm.at[:, pl.ds(chunk * w_rows, w_rows), :], raw_w.at[chunk], raw_sem.at[chunk]
        ).wait()
        for which in range(3):
            for half in range(2):
                place = pl.multiple_of((half ^ high) * (3 * LANES) + which * LANES, LANES)
                both_w[core, pl.ds(pl.multiple_of(chunk * w_rows, w_rows), w_rows), pl.ds(place, LANES)] = (
                    raw_w[chunk, which, :, half * LANES : (half + 1) * LANES].astype(F32).astype(BF16)
                )

    pl.semaphore_wait(barrier, devices - 1)

    home = x * 4 + y
    far_copy = pltpu.make_async_remote_copy(
        src_ref=own_x, dst_ref=all_x.at[home, core], send_sem=first_send.at[0],
        recv_sem=first_recv.at[core],
        device_id=device(x, y, 1 - layer, high, layer), device_id_type=MESH,
    )
    far_copy.start()
    near_copy = pltpu.make_async_remote_copy(
        src_ref=own_x, dst_ref=all_x.at[home, core], send_sem=first_send.at[1],
        recv_sem=first_recv.at[core],
        device_id=device(x, y, layer, high, layer), device_id_type=MESH,
    )
    local_copy = pltpu.make_async_copy(own_x, all_x.at[home, core], first_recv.at[core])

    @pl.when(core == layer)
    def _():
        local_copy.start()

    @pl.when(core != layer)
    def _():
        near_copy.start()

    sibling = device(x, y, layer, high, 1 - core)

    def w_copy(chunk):
        piece = both_w.at[core, pl.ds(pl.multiple_of(chunk * w_rows, w_rows), w_rows), :]
        return pltpu.make_async_remote_copy(
            src_ref=piece, dst_ref=piece, send_sem=w_send.at[chunk], recv_sem=w_recv.at[chunk],
            device_id=sibling, device_id_type=MESH,
        )

    def w_arrival(chunk):
        piece = both_w.at[1 - core, pl.ds(pl.multiple_of(chunk * w_rows, w_rows), w_rows), :]
        return pltpu.make_async_remote_copy(
            src_ref=piece, dst_ref=piece, send_sem=w_send.at[chunk], recv_sem=w_recv.at[chunk],
            device_id=sibling, device_id_type=MESH,
        )

    def piece_of(axis, group, along):
        shifted = jnp.maximum(group - 1, 0)
        first = jnp.where(group == 0, 1, 0)
        if axis == 0:
            return wrap(x + along) * 4 + wrap(y + shifted), 1 - first
        return wrap(x + shifted) * 4 + wrap(y + along), first

    def ring_copy(axis, way, group, turn, along, feat):
        slot, part = piece_of(axis, group, along)
        unit = all_x.at[slot, feat, pl.ds(pl.multiple_of(part * half_rows, half_rows), half_rows), :]
        step = 1 if way == 0 else -1
        target = (
            device(wrap(x + step), y, layer, high, core)
            if axis == 0
            else device(x, wrap(y + step), layer, high, core)
        )
        return pltpu.make_async_remote_copy(
            src_ref=unit, dst_ref=unit,
            send_sem=ring_send.at[axis, way, group * 3 + turn],
            recv_sem=ring_recv.at[axis, way, group * 3 + turn],
            device_id=target, device_id_type=MESH,
        )

    def send_own(group):
        for turn in range(2):
            for axis in range(2):
                for way in range(2):
                    ring_copy(axis, way, group, turn, 0, turn ^ way).start()

    def send_on(group):
        for axis in range(2):
            for way in range(2):
                ring_copy(axis, way, group, 2, -1 if way == 0 else 1, way).start()

    def wait_own(group):
        for turn in range(2):
            for axis in range(2):
                for way in range(2):
                    ring_copy(axis, way, group, turn, -1 if way == 0 else 1, turn ^ way).wait_recv()

    def wait_on(group):
        for axis in range(2):
            for way in range(2):
                ring_copy(axis, way, group, 2, 2, way).wait_recv()

    far_home = device(x, y, layer, 1 - high, core)

    def far_copy_of(row):
        return pltpu.make_async_remote_copy(
            src_ref=sums.at[pl.ds(row, half_rows), pl.ds(3 * LANES, 3 * LANES)],
            dst_ref=far_sums.at[pl.ds(row, half_rows), :],
            send_sem=far_send.at[row // half_rows], recv_sem=far_recv,
            device_id=far_home, device_id_type=MESH,
        )

    def multiply(pieces):
        total = None
        for feat in range(2):
            left = jnp.concatenate(
                [
                    all_x[slot, feat, pl.ds(pl.multiple_of(part * half_rows, half_rows), half_rows), :]
                    for slot, part in pieces
                ],
                axis=0,
            )
            term = jnp.dot(left, both_w[feat], preferred_element_type=F32)
            total = term if total is None else total + term
        for index, (slot, part) in enumerate(pieces):
            row = pl.multiple_of(slot * rows + part * half_rows, half_rows)
            sums[pl.ds(row, half_rows), :] = total[index * half_rows : (index + 1) * half_rows]
        for slot, part in pieces:
            far_copy_of(pl.multiple_of(slot * rows + part * half_rows, half_rows)).start()

    @pl.loop(0, w_chunks)
    def _(chunk):
        convert_chunk(chunk)
        w_copy(chunk).start()

    for feat in range(2):
        landed = all_x.at[home, feat]
        pltpu.make_async_copy(landed, landed, first_recv.at[feat]).wait()
    send_own(0)
    send_own(1)

    @pl.loop(0, GROUPS)
    def _(group):
        wait_own(group)
        send_on(group)

        @pl.when(group == 0)
        def _():
            @pl.loop(0, w_chunks)
            def _(chunk):
                w_arrival(chunk).wait_recv()

        multiply(
            [piece_of(0, group, -1), piece_of(0, group, 1), piece_of(1, group, -1), piece_of(1, group, 1)]
        )

        @pl.when(group > 0)
        def _():
            wait_on(group - 1)

        @pl.when(group + 2 < GROUPS)
        def _():
            send_own(group + 2)

        before = jnp.maximum(group - 1, 0)
        slot_x, part_x = piece_of(0, before, 2)
        slot_y, part_y = piece_of(1, before, 2)
        start = group == 0
        multiply(
            [
                (jnp.where(start, home, slot_x), jnp.where(start, 0, part_x)),
                (jnp.where(start, home, slot_y), jnp.where(start, 1, part_y)),
            ]
        )

    wait_on(GROUPS - 1)
    multiply([piece_of(0, GROUPS - 1, 2), piece_of(1, GROUPS - 1, 2)])

    requant = halves_of(high, mult_ref[...].astype(F32) * jnp.exp2(-shift_ref[...].astype(F32)))
    taps = halves_of(high, short_ref[...].astype(F32) * (1.0 / 8192.0))
    rates = halves_of(high, rates_ref[...])
    coeffs = (
        halves_of(high, residue_ref[...].astype(F32))
        * (1.0 / (127.0 * math.sqrt(modes)))
        * jnp.sqrt(small_expm1_neg(2.0 * rates))
    )
    skip = halves_of(high, skip_ref[...])
    decays = jnp.exp(-rates)
    chunk_decays = jnp.exp(-rates * float(step_count))

    pltpu.make_async_copy(far_sums, far_sums, far_recv).wait()

    @pl.loop(0, coded.shape[1] // rows)
    def _(block):
        at = pl.ds(pl.multiple_of(block * rows, rows), rows)
        for which in range(3):
            lanes = slice(which * LANES, (which + 1) * LANES)
            total = (sums[at, lanes] + far_sums[at, lanes]) * requant[which : which + 1, :]
            coded[which, at, :] = jnp.clip(total, -127.0, 127.0).astype(BF16).astype(F32)

    for back in range(2):
        for which in range(3):
            tails[back, which] = coded[which, pl.ds(step_count - 1 - back, CHUNKS, stride=step_count), :]
    tail_copy = pltpu.make_async_remote_copy(
        src_ref=tails, dst_ref=sib_tails, send_sem=tail_send, recv_sem=tail_recv,
        device_id=sibling, device_id_type=MESH,
    )
    tail_copy.start()

    def spread(row):
        return jnp.broadcast_to(row, (CHUNKS, LANES))

    tap_rows = [[spread(taps[lag, which : which + 1, :]) for which in range(3)] for lag in range(3)]
    decay_rows = [spread(decays[mode : mode + 1, :]) for mode in range(modes)]
    tail_copy.wait_recv()
    index = lax.broadcasted_iota(jnp.int32, (CHUNKS, LANES), 0)
    odd = lax.rem(index, 2) == 1

    def before_chunk(back, which):
        own = pltpu.roll(tails[back, which], 1, 0)
        other = sib_tails[back, which]
        up = pltpu.roll(other, 1, 0)
        down = pltpu.roll(other, CHUNKS - 1, 0)
        outside = jnp.where(core == 0, jnp.where(index == 0, 0.0, up), down)
        return jnp.where(odd, own, outside)

    def first_pass(step, carry):
        older, newer, states = carry
        now = [coded[which, pl.ds(step, CHUNKS, stride=step_count), :] for which in range(3)]
        feat = [
            tap_rows[0][which] * now[which]
            + tap_rows[1][which] * newer[which]
            + tap_rows[2][which] * older[which]
            for which in range(3)
        ]
        drive = feat[1] * feat[2]
        at = pl.ds(pl.multiple_of(step * CHUNKS, CHUNKS), CHUNKS)
        queries[at, :] = feat[0]
        drives[at, :] = drive
        states = tuple(decay_rows[mode] * states[mode] + drive for mode in range(modes))
        return tuple(newer), tuple(now), states

    zero = jnp.zeros((CHUNKS, LANES), F32)
    carry = (
        tuple(before_chunk(1, which) for which in range(3)),
        tuple(before_chunk(0, which) for which in range(3)),
        tuple(zero for _ in range(modes)),
    )
    _, _, states = lax.fori_loop(0, step_count, first_pass, carry, unroll=4)
    for mode in range(modes):
        ends[mode * CHUNKS : (mode + 1) * CHUNKS, :] = states[mode]
    end_copy = pltpu.make_async_remote_copy(
        src_ref=ends, dst_ref=sib_ends, send_sem=end_send, recv_sem=end_recv,
        device_id=sibling, device_id_type=MESH,
    )
    end_copy.start()
    coeff_rows = [spread(coeffs[mode : mode + 1, :]) for mode in range(modes)]
    skip_row = spread(skip)
    end_copy.wait_recv()
    state = jnp.zeros((modes, LANES), F32)
    for run in range(CHUNKS // 2):
        for owner in range(2):
            for chunk in (2 * run, 2 * run + 1):
                rows_at = pl.ds(chunk, modes, stride=CHUNKS)
                starts[owner, rows_at, :] = state
                ended = jnp.where(core == owner, ends[rows_at, :], sib_ends[rows_at, :])
                state = chunk_decays * state + ended

    out_rows = out_ref.shape[0]
    blocks = step_count // out_rows
    channel = pl.multiple_of((seq * 2 + high) * LANES, LANES)

    def second_pass(step, states):
        at = pl.ds(pl.multiple_of(step * CHUNKS, CHUNKS), CHUNKS)
        drive = drives[at, :]
        states = tuple(decay_rows[mode] * states[mode] + drive for mode in range(modes))
        parts = [coeff_rows[mode] * states[mode] for mode in range(modes)]
        while len(parts) > 1:
            parts = [parts[i] + parts[i + 1] for i in range(0, len(parts), 2)]
        gated[at, :] = queries[at, :] * (parts[0] + skip_row * drive)
        return states

    def out_copies(block, chunk):
        target = device(chunk // 2, (chunk % 2) * 2 + block // 4, core, lax.rem(block, 4) // 2, lax.rem(block, 2))
        source = staged.at[block, chunk]
        place = out_ref.at[:, pl.ds(channel, LANES)]
        remote = pltpu.make_async_remote_copy(
            src_ref=source, dst_ref=place, send_sem=out_send.at[block, chunk], recv_sem=out_recv,
            device_id=target, device_id_type=MESH,
        )
        local = pltpu.make_async_copy(source, place, out_recv)
        is_me = jnp.logical_and(target[0] == seq, target[1] == tp)
        return is_me, remote, local

    def out_block(block, states):
        states = lax.fori_loop(
            0, out_rows, lambda step, held: second_pass(block * out_rows + step, held), states, unroll=4
        )
        for chunk in range(CHUNKS):
            taken = gated[pl.ds(block * (out_rows * CHUNKS) + chunk, out_rows, stride=CHUNKS), :]
            staged[block, chunk] = taken.astype(BF16)
        for chunk in range(CHUNKS):
            is_me, remote, local = out_copies(block, chunk)

            @pl.when(is_me)
            def _():
                local.start()

            @pl.when(jnp.logical_not(is_me))
            def _():
                remote.start()

        return states

    states = tuple(starts[core, mode * CHUNKS : (mode + 1) * CHUNKS, :] for mode in range(modes))
    lax.fori_loop(0, blocks, out_block, states)

    far_copy.wait_send()

    @pl.when(core != layer)
    def _():
        near_copy.wait_send()

    @pl.loop(0, w_chunks)
    def _(chunk):
        w_copy(chunk).wait_send()

    @pl.loop(0, GROUPS)
    def _(group):
        for turn in range(3):
            for axis in range(2):
                for way in range(2):
                    ring_copy(axis, way, group, turn, 0, 0).wait_send()

    @pl.loop(0, sums.shape[0] // half_rows)
    def _(block):
        far_copy_of(pl.multiple_of(block * half_rows, half_rows)).wait_send()

    tail_copy.wait_send()
    end_copy.wait_send()

    @pl.loop(0, blocks)
    def _(block):
        for chunk in range(CHUNKS):
            is_me, remote, _ = out_copies(block, chunk)

            @pl.when(jnp.logical_not(is_me))
            def _():
                remote.wait_send()

    pltpu.make_async_copy(out_ref, out_ref, out_recv).wait()


def on_device(x_codes, w_codes, req_mult, req_shift, short_codes, residue_codes, rates, skip_gain):
    rows, feats = x_codes.shape
    seq_devs = lax.axis_size("seq")
    tp_devs = lax.axis_size("tp")
    cols = w_codes.shape[2]
    positions = rows * seq_devs // 2
    modes = residue_codes.shape[0]
    out_rows = rows // tp_devs
    steps = positions // CHUNKS
    blocks = steps // out_rows
    w_rows = 256
    w_chunks = feats // w_rows
    vmem = pl.BlockSpec(memory_space=pltpu.VMEM)
    dma = pltpu.SemaphoreType.DMA
    return pl.pallas_call(
        hyena_kernel,
        out_shape=jax.ShapeDtypeStruct((out_rows, cols * seq_devs), BF16),
        in_specs=[vmem, pl.BlockSpec(memory_space=pl.ANY)] + [vmem] * 6,
        out_specs=vmem,
        scratch_shapes=[
            pltpu.VMEM((rows, feats), BF16),
            pltpu.VMEM((seq_devs // 2, 2, rows, feats), BF16),
            pltpu.VMEM((w_chunks, 3, w_rows, cols), jnp.int32),
            pltpu.VMEM((2, feats, 3 * cols), BF16),
            pltpu.VMEM((positions, 3 * cols), F32),
            pltpu.VMEM((positions, 3 * LANES), F32),
            pltpu.VMEM((3, positions, LANES), F32),
            pltpu.VMEM((2, 3, CHUNKS, LANES), F32),
            pltpu.VMEM((2, 3, CHUNKS, LANES), F32),
            pltpu.VMEM((modes * CHUNKS, LANES), F32),
            pltpu.VMEM((modes * CHUNKS, LANES), F32),
            pltpu.VMEM((2, modes * CHUNKS, LANES), F32),
            pltpu.VMEM((positions, LANES), F32),
            pltpu.VMEM((positions, LANES), F32),
            pltpu.VMEM((positions, LANES), F32),
            pltpu.VMEM((blocks, CHUNKS, out_rows, LANES), BF16),
            dma((2,)),
            dma((2,)),
            dma((w_chunks,)),
            dma((w_chunks,)),
            dma((w_chunks,)),
            dma((2, 2, 3 * GROUPS)),
            dma((2, 2, 3 * GROUPS)),
            dma((positions // (rows // 2),)),
            dma,
            dma,
            dma,
            dma,
            dma,
            dma((blocks, CHUNKS)),
            dma,
        ],
        compiler_params=pltpu.CompilerParams(
            collective_id=0, has_side_effects=True, vmem_limit_bytes=64 * 1024 * 1024 - 65536
        ),
    )(x_codes, w_codes, req_mult, req_shift, short_codes, residue_codes, rates, skip_gain.reshape(1, -1))


def solution(mesh):
    placed = (
        P("seq", "tp"),
        P(None, "tp", "seq"),
        P(None, "seq"),
        P(None, "seq"),
        P(None, None, "seq"),
        P(None, "seq"),
        P(None, "seq"),
        P("seq"),
    )
    return jax.shard_map(
        on_device, mesh=mesh, in_specs=placed, out_specs=P(("seq", "tp"), None), check_vma=False
    )
```

```python
import functools
import math

import jax
import jax.numpy as jnp
from jax import lax
from jax.experimental import pallas as pl
from jax.experimental.pallas import tpu as pltpu
from jax.sharding import PartitionSpec as P

MESH = pl.DeviceIdType.MESH
F32 = jnp.float32
BF16 = jnp.bfloat16
LANES = 128
CHUNKS = 8
RING = 4
GROUPS = 5


def halves_of(which, array):
    return jnp.where(which == 0, array[..., :LANES], array[..., LANES:])


def small_expm1_neg(z):
    poly = jnp.ones_like(z)
    for order in range(8, 1, -1):
        poly = 1.0 - (z * (1.0 / order)) * poly
    return z * poly


def hyena_kernel(
    x_hbm, w_hbm, mult_ref, shift_ref, short_ref, residue_ref, rates_ref, skip_ref,
    out_ref,
    raw_x, own_x, all_x, raw_w, both_w, sums, near_codes, near_steps, far_codes, far_steps, coded, tails, sib_tails, ends, sib_ends,
    starts, queries, drives, gated, staged,
    x_sem, first_send, first_recv, raw_sem, w_send, w_recv, ring_send, ring_recv,
    far_send, far_recv, step_send, step_recv, tail_send, tail_recv, end_send, end_recv, out_send, out_recv,
):
    seq = lax.axis_index("seq")
    tp = lax.axis_index("tp")
    y = lax.rem(seq, 4)
    layer = lax.rem(seq // 4, 2)
    x = seq // 8
    core = lax.rem(tp, 2)
    high = tp // 2
    rows, feats = own_x.shape
    half_rows = rows // 2
    modes = residue_ref.shape[0]
    step_count = coded.shape[1] // CHUNKS

    def device(x_at, y_at, layer_at, high_at, core_at):
        return ((x_at * 2 + layer_at) * 4 + y_at, high_at * 2 + core_at)

    def wrap(value):
        return lax.rem(value + 2 * RING, RING)

    raw_copy = pltpu.make_async_copy(x_hbm, raw_x, x_sem)
    raw_copy.start()
    w_chunks = raw_w.shape[0]
    w_rows = raw_w.shape[2]
    for chunk in range(w_chunks):
        pltpu.make_async_copy(
            w_hbm.at[:, pl.ds(chunk * w_rows, w_rows), :], raw_w.at[chunk], raw_sem.at[chunk]
        ).start()

    barrier = pltpu.get_barrier_semaphore()
    column = layer * 2 + high * 4 + core

    def greet(target):
        pl.semaphore_signal(barrier, inc=1, device_id=target, device_id_type=MESH)

    for offset in range(1, 8):
        other = lax.rem(column + offset, 8)
        greet(device(x, y, lax.rem(other // 2, 2), other // 4, lax.rem(other, 2)))
    for step in (1, RING - 1):
        greet(device(wrap(x + step), y, layer, high, core))
        greet(device(x, wrap(y + step), layer, high, core))

    raw_copy.wait()
    own_x[...] = raw_x[...].astype(F32).astype(BF16)

    def convert_chunk(chunk):
        pltpu.make_async_copy(
            w_hbm.at[:, pl.ds(chunk * w_rows, w_rows), :], raw_w.at[chunk], raw_sem.at[chunk]
        ).wait()
        for which in range(3):
            for half in range(2):
                place = pl.multiple_of((half ^ high) * (3 * LANES) + which * LANES, LANES)
                both_w[core, pl.ds(pl.multiple_of(chunk * w_rows, w_rows), w_rows), pl.ds(place, LANES)] = (
                    raw_w[chunk, which, :, half * LANES : (half + 1) * LANES].astype(F32).astype(BF16)
                )

    pl.semaphore_wait(barrier, 11)

    home = x * 4 + y

    def first_copy(part, target_layer, turn):
        at = pl.ds(part * half_rows, half_rows)
        return pltpu.make_async_remote_copy(
            src_ref=own_x.at[at, :], dst_ref=all_x.at[home, core, at, :],
            send_sem=first_send.at[turn, part], recv_sem=first_recv.at[core, part],
            device_id=device(x, y, target_layer, high, layer), device_id_type=MESH,
        )

    for part in range(2):
        first_copy(part, 1 - layer, 0).start()

        @pl.when(core == layer)
        def _():
            at = pl.ds(part * half_rows, half_rows)
            pltpu.make_async_copy(
                own_x.at[at, :], all_x.at[home, core, at, :], first_recv.at[core, part]
            ).start()

        @pl.when(core != layer)
        def _():
            first_copy(part, layer, 1).start()

    sibling = device(x, y, layer, high, 1 - core)

    def w_copy(chunk):
        piece = both_w.at[core, pl.ds(pl.multiple_of(chunk * w_rows, w_rows), w_rows), :]
        return pltpu.make_async_remote_copy(
            src_ref=piece, dst_ref=piece, send_sem=w_send.at[chunk], recv_sem=w_recv.at[chunk],
            device_id=sibling, device_id_type=MESH,
        )

    def w_arrival(chunk):
        piece = both_w.at[1 - core, pl.ds(pl.multiple_of(chunk * w_rows, w_rows), w_rows), :]
        return pltpu.make_async_remote_copy(
            src_ref=piece, dst_ref=piece, send_sem=w_send.at[chunk], recv_sem=w_recv.at[chunk],
            device_id=sibling, device_id_type=MESH,
        )

    def piece_of(axis, group, along):
        shifted = jnp.maximum(group - 1, 0)
        first = jnp.where(group == 0, 1, 0)
        if axis == 0:
            return wrap(x + along) * 4 + wrap(y + shifted), 1 - first
        return wrap(x + shifted) * 4 + wrap(y + along), first

    def ring_copy(axis, way, group, turn, along, feat):
        slot, part = piece_of(axis, group, along)
        unit = all_x.at[slot, feat, pl.ds(pl.multiple_of(part * half_rows, half_rows), half_rows), :]
        step = 1 if way == 0 else -1
        target = (
            device(wrap(x + step), y, layer, high, core)
            if axis == 0
            else device(x, wrap(y + step), layer, high, core)
        )
        return pltpu.make_async_remote_copy(
            src_ref=unit, dst_ref=unit,
            send_sem=ring_send.at[axis, way, group * 3 + turn],
            recv_sem=ring_recv.at[axis, way, group * 3 + turn],
            device_id=target, device_id_type=MESH,
        )

    def send_own(group):
        for turn in range(2):
            for axis in range(2):
                for way in range(2):
                    ring_copy(axis, way, group, turn, 0, turn ^ way).start()

    def send_on(group):
        for axis in range(2):
            for way in range(2):
                ring_copy(axis, way, group, 2, -1 if way == 0 else 1, way).start()

    def wait_own(group):
        for turn in range(2):
            for axis in range(2):
                for way in range(2):
                    ring_copy(axis, way, group, turn, -1 if way == 0 else 1, turn ^ way).wait_recv()

    def wait_on(group):
        for axis in range(2):
            for way in range(2):
                ring_copy(axis, way, group, 2, 2, way).wait_recv()

    far_home = device(x, y, layer, 1 - high, core)

    def far_copies(row):
        piece = row // half_rows
        return (
            pltpu.make_async_remote_copy(
                src_ref=near_codes.at[piece], dst_ref=far_codes.at[piece],
                send_sem=far_send.at[piece], recv_sem=far_recv,
                device_id=far_home, device_id_type=MESH,
            ),
            pltpu.make_async_remote_copy(
                src_ref=near_steps.at[piece], dst_ref=far_steps.at[piece],
                send_sem=step_send.at[piece], recv_sem=step_recv,
                device_id=far_home, device_id_type=MESH,
            ),
        )

    def multiply(pieces):
        total = None
        for feat in range(2):
            left = jnp.concatenate(
                [
                    all_x[slot, feat, pl.ds(pl.multiple_of(part * half_rows, half_rows), half_rows), :]
                    for slot, part in pieces
                ],
                axis=0,
            )
            term = jnp.dot(left, both_w[feat], preferred_element_type=F32)
            total = term if total is None else total + term
        for index, (slot, part) in enumerate(pieces):
            row = pl.multiple_of(slot * rows + part * half_rows, half_rows)
            part_sums = total[index * half_rows : (index + 1) * half_rows]
            sums[pl.ds(row, half_rows), :] = part_sums[:, : 3 * LANES]
            away = part_sums[:, 3 * LANES :]
            peak = jnp.maximum(jnp.max(jnp.abs(away), axis=0, keepdims=True), 1.0)
            near_steps[row // half_rows] = peak * (1.0 / 32767.0)
            scaled = jnp.round(away * (32767.0 / peak))
            near_codes[row // half_rows] = scaled.astype(jnp.int32).astype(jnp.int16)
        for slot, part in pieces:
            for copy in far_copies(slot * rows + part * half_rows):
                copy.start()

    def begin_ring():
        for part in range(2):
            for feat in range(2):
                landed = all_x.at[home, feat, pl.ds(part * half_rows, half_rows), :]
                pltpu.make_async_copy(landed, landed, first_recv.at[feat, part]).wait()
        send_own(0)
        send_own(1)

    @pl.when(core == layer)
    def _():
        begin_ring()

    @pl.loop(0, w_chunks)
    def _(chunk):
        convert_chunk(chunk)
        w_copy(chunk).start()

    @pl.when(core != layer)
    def _():
        begin_ring()

    @pl.loop(0, GROUPS)
    def _(group):
        wait_own(group)
        send_on(group)

        @pl.when(group == 0)
        def _():
            @pl.loop(0, w_chunks)
            def _(chunk):
                w_arrival(chunk).wait_recv()

        multiply(
            [piece_of(0, group, -1), piece_of(0, group, 1), piece_of(1, group, -1), piece_of(1, group, 1)]
        )

        @pl.when(group > 0)
        def _():
            wait_on(group - 1)

        @pl.when(group + 2 < GROUPS)
        def _():
            send_own(group + 2)

        before = jnp.maximum(group - 1, 0)
        slot_x, part_x = piece_of(0, before, 2)
        slot_y, part_y = piece_of(1, before, 2)
        start = group == 0
        multiply(
            [
                (jnp.where(start, home, slot_x), jnp.where(start, 0, part_x)),
                (jnp.where(start, home, slot_y), jnp.where(start, 1, part_y)),
            ]
        )

    wait_on(GROUPS - 1)
    multiply([piece_of(0, GROUPS - 1, 2), piece_of(1, GROUPS - 1, 2)])

    requant = halves_of(high, mult_ref[...].astype(F32) * jnp.exp2(-shift_ref[...].astype(F32)))
    taps = halves_of(high, short_ref[...].astype(F32) * (1.0 / 8192.0))
    rates = halves_of(high, rates_ref[...])
    coeffs = (
        halves_of(high, residue_ref[...].astype(F32))
        * (1.0 / (127.0 * math.sqrt(modes)))
        * jnp.sqrt(small_expm1_neg(2.0 * rates))
    )
    skip = halves_of(high, skip_ref[...])
    decays = jnp.exp(-rates)
    chunk_decays = jnp.exp(-rates * float(step_count))

    pltpu.make_async_copy(far_codes, far_codes, far_recv).wait()
    pltpu.make_async_copy(far_steps, far_steps, step_recv).wait()

    @pl.loop(0, far_codes.shape[0])
    def _(piece):
        at = pl.ds(pl.multiple_of(piece * half_rows, half_rows), half_rows)
        for which in range(3):
            lanes = slice(which * LANES, (which + 1) * LANES)
            away = far_codes[piece, :, lanes].astype(jnp.int32).astype(F32) * far_steps[piece, :, lanes]
            total = (sums[at, lanes] + away) * requant[which : which + 1, :]
            coded[which, at, :] = jnp.clip(total, -127.0, 127.0).astype(BF16).astype(F32)

    for back in range(2):
        for which in range(3):
            tails[back, which] = coded[which, pl.ds(step_count - 1 - back, CHUNKS, stride=step_count), :]
    tail_copy = pltpu.make_async_remote_copy(
        src_ref=tails, dst_ref=sib_tails, send_sem=tail_send, recv_sem=tail_recv,
        device_id=sibling, device_id_type=MESH,
    )
    tail_copy.start()

    def spread(row):
        return jnp.broadcast_to(row, (CHUNKS, LANES))

    tap_rows = [[spread(taps[lag, which : which + 1, :]) for which in range(3)] for lag in range(3)]
    decay_rows = [spread(decays[mode : mode + 1, :]) for mode in range(modes)]
    tail_copy.wait_recv()
    index = lax.broadcasted_iota(jnp.int32, (CHUNKS, LANES), 0)
    odd = lax.rem(index, 2) == 1

    def before_chunk(back, which):
        own = pltpu.roll(tails[back, which], 1, 0)
        other = sib_tails[back, which]
        up = pltpu.roll(other, 1, 0)
        down = pltpu.roll(other, CHUNKS - 1, 0)
        outside = jnp.where(core == 0, jnp.where(index == 0, 0.0, up), down)
        return jnp.where(odd, own, outside)

    def first_pass(step, carry):
        older, newer, states = carry
        now = [coded[which, pl.ds(step, CHUNKS, stride=step_count), :] for which in range(3)]
        feat = [
            tap_rows[0][which] * now[which]
            + tap_rows[1][which] * newer[which]
            + tap_rows[2][which] * older[which]
            for which in range(3)
        ]
        drive = feat[1] * feat[2]
        at = pl.ds(pl.multiple_of(step * CHUNKS, CHUNKS), CHUNKS)
        queries[at, :] = feat[0]
        drives[at, :] = drive
        states = tuple(decay_rows[mode] * states[mode] + drive for mode in range(modes))
        return tuple(newer), tuple(now), states

    zero = jnp.zeros((CHUNKS, LANES), F32)
    carry = (
        tuple(before_chunk(1, which) for which in range(3)),
        tuple(before_chunk(0, which) for which in range(3)),
        tuple(zero for _ in range(modes)),
    )
    _, _, states = lax.fori_loop(0, step_count, first_pass, carry, unroll=4)
    for mode in range(modes):
        ends[mode * CHUNKS : (mode + 1) * CHUNKS, :] = states[mode]
    end_copy = pltpu.make_async_remote_copy(
        src_ref=ends, dst_ref=sib_ends, send_sem=end_send, recv_sem=end_recv,
        device_id=sibling, device_id_type=MESH,
    )
    end_copy.start()
    coeff_rows = [spread(coeffs[mode : mode + 1, :]) for mode in range(modes)]
    skip_row = spread(skip)
    end_copy.wait_recv()
    state = jnp.zeros((modes, LANES), F32)
    for run in range(CHUNKS // 2):
        for owner in range(2):
            for chunk in (2 * run, 2 * run + 1):
                rows_at = pl.ds(chunk, modes, stride=CHUNKS)
                starts[owner, rows_at, :] = state
                ended = jnp.where(core == owner, ends[rows_at, :], sib_ends[rows_at, :])
                state = chunk_decays * state + ended

    out_rows = out_ref.shape[0]
    blocks = step_count // out_rows
    channel = pl.multiple_of((seq * 2 + high) * LANES, LANES)

    def second_pass(step, states):
        at = pl.ds(pl.multiple_of(step * CHUNKS, CHUNKS), CHUNKS)
        drive = drives[at, :]
        states = tuple(decay_rows[mode] * states[mode] + drive for mode in range(modes))
        parts = [coeff_rows[mode] * states[mode] for mode in range(modes)]
        while len(parts) > 1:
            parts = [parts[i] + parts[i + 1] for i in range(0, len(parts), 2)]
        gated[at, :] = queries[at, :] * (parts[0] + skip_row * drive)
        return states

    def out_copies(block, chunk):
        target = device(chunk // 2, (chunk % 2) * 2 + block // 4, core, lax.rem(block, 4) // 2, lax.rem(block, 2))
        source = staged.at[block, chunk]
        place = out_ref.at[:, pl.ds(channel, LANES)]
        remote = pltpu.make_async_remote_copy(
            src_ref=source, dst_ref=place, send_sem=out_send.at[block, chunk], recv_sem=out_recv,
            device_id=target, device_id_type=MESH,
        )
        local = pltpu.make_async_copy(source, place, out_recv)
        is_me = jnp.logical_and(target[0] == seq, target[1] == tp)
        return is_me, remote, local

    def out_block(block, states):
        states = lax.fori_loop(
            0, out_rows, lambda step, held: second_pass(block * out_rows + step, held), states, unroll=4
        )
        for chunk in range(CHUNKS):
            taken = gated[pl.ds(block * (out_rows * CHUNKS) + chunk, out_rows, stride=CHUNKS), :]
            staged[block, chunk] = taken.astype(BF16)
        for chunk in range(CHUNKS):
            is_me, remote, local = out_copies(block, chunk)

            @pl.when(is_me)
            def _():
                local.start()

            @pl.when(jnp.logical_not(is_me))
            def _():
                remote.start()

        return states

    states = tuple(starts[core, mode * CHUNKS : (mode + 1) * CHUNKS, :] for mode in range(modes))
    lax.fori_loop(0, blocks, out_block, states)

    for part in range(2):
        first_copy(part, 1 - layer, 0).wait_send()

        @pl.when(core != layer)
        def _():
            first_copy(part, layer, 1).wait_send()

    @pl.loop(0, w_chunks)
    def _(chunk):
        w_copy(chunk).wait_send()

    @pl.loop(0, GROUPS)
    def _(group):
        for turn in range(3):
            for axis in range(2):
                for way in range(2):
                    ring_copy(axis, way, group, turn, 0, 0).wait_send()

    @pl.loop(0, near_codes.shape[0])
    def _(piece):
        for copy in far_copies(piece * half_rows):
            copy.wait_send()

    tail_copy.wait_send()
    end_copy.wait_send()

    @pl.loop(0, blocks)
    def _(block):
        for chunk in range(CHUNKS):
            is_me, remote, _ = out_copies(block, chunk)

            @pl.when(jnp.logical_not(is_me))
            def _():
                remote.wait_send()

    pltpu.make_async_copy(out_ref, out_ref, out_recv).wait()


def on_device(x_codes, w_codes, req_mult, req_shift, short_codes, residue_codes, rates, skip_gain):
    rows, feats = x_codes.shape
    seq_devs = lax.axis_size("seq")
    tp_devs = lax.axis_size("tp")
    cols = w_codes.shape[2]
    positions = rows * seq_devs // 2
    modes = residue_codes.shape[0]
    out_rows = rows // tp_devs
    steps = positions // CHUNKS
    blocks = steps // out_rows
    pieces = 2 * positions // rows
    w_rows = 256
    w_chunks = feats // w_rows
    vmem = pl.BlockSpec(memory_space=pltpu.VMEM)
    dma = pltpu.SemaphoreType.DMA
    return pl.pallas_call(
        hyena_kernel,
        out_shape=jax.ShapeDtypeStruct((out_rows, cols * seq_devs), BF16),
        in_specs=[pl.BlockSpec(memory_space=pl.ANY)] * 2 + [vmem] * 6,
        out_specs=pl.BlockSpec(memory_space=pl.ANY),
        scratch_shapes=[
            pltpu.VMEM((rows, feats), jnp.int32),
            pltpu.VMEM((rows, feats), BF16),
            pltpu.VMEM((seq_devs // 2, 2, rows, feats), BF16),
            pltpu.VMEM((w_chunks, 3, w_rows, cols), jnp.int32),
            pltpu.VMEM((2, feats, 3 * cols), BF16),
            pltpu.VMEM((positions, 3 * LANES), F32),
            pltpu.VMEM((pieces, rows // 2, 3 * LANES), jnp.int16),
            pltpu.VMEM((pieces, 1, 3 * LANES), F32),
            pltpu.VMEM((pieces, rows // 2, 3 * LANES), jnp.int16),
            pltpu.VMEM((pieces, 1, 3 * LANES), F32),
            pltpu.VMEM((3, positions, LANES), F32),
            pltpu.VMEM((2, 3, CHUNKS, LANES), F32),
            pltpu.VMEM((2, 3, CHUNKS, LANES), F32),
            pltpu.VMEM((modes * CHUNKS, LANES), F32),
            pltpu.VMEM((modes * CHUNKS, LANES), F32),
            pltpu.VMEM((2, modes * CHUNKS, LANES), F32),
            pltpu.VMEM((positions, LANES), F32),
            pltpu.VMEM((positions, LANES), F32),
            pltpu.VMEM((positions, LANES), F32),
            pltpu.VMEM((blocks, CHUNKS, out_rows, LANES), BF16),
            dma,
            dma((2, 2)),
            dma((2, 2)),
            dma((w_chunks,)),
            dma((w_chunks,)),
            dma((w_chunks,)),
            dma((2, 2, 3 * GROUPS)),
            dma((2, 2, 3 * GROUPS)),
            dma((pieces,)),
            dma,
            dma((pieces,)),
            dma,
            dma,
            dma,
            dma,
            dma,
            dma((blocks, CHUNKS)),
            dma,
        ],
        compiler_params=pltpu.CompilerParams(
            collective_id=0, has_side_effects=True, vmem_limit_bytes=64 * 1024 * 1024 - 65536
        ),
    )(x_codes, w_codes, req_mult, req_shift, short_codes, residue_codes, rates, skip_gain.reshape(1, -1))


def solution(mesh):
    placed = (
        P("seq", "tp"),
        P(None, "tp", "seq"),
        P(None, "seq"),
        P(None, "seq"),
        P(None, None, "seq"),
        P(None, "seq"),
        P(None, "seq"),
        P("seq"),
    )
    return jax.shard_map(
        on_device, mesh=mesh, in_specs=placed, out_specs=P(("seq", "tp"), None), check_vma=False
    )
```

```python
import functools
import math

import jax
import jax.numpy as jnp
from jax import lax
from jax.experimental import pallas as pl
from jax.experimental.pallas import tpu as pltpu
from jax.sharding import PartitionSpec as P

MESH = pl.DeviceIdType.MESH
F32 = jnp.float32
BF16 = jnp.bfloat16
LANES = 128
CHUNKS = 8
RING = 4
GROUPS = 5
LATE = 384


def halves_of(which, array):
    return jnp.where(which == 0, array[..., :LANES], array[..., LANES:])


def small_expm1_neg(z):
    poly = jnp.ones_like(z)
    for order in range(8, 1, -1):
        poly = 1.0 - (z * (1.0 / order)) * poly
    return z * poly


def hyena_kernel(
    x_hbm, w_hbm, mult_ref, shift_ref, short_ref, residue_ref, rates_ref, skip_ref,
    out_ref,
    raw_x, own_x, all_x, raw_w, both_w, sums, near_codes, near_steps, far_codes, far_steps, coded, tails, sib_tails, ends, sib_ends,
    starts, queries, drives, gated, staged,
    x_sem, first_send, first_recv, raw_sem, w_send, w_recv, ring_send, ring_recv, late_send, late_recv,
    far_send, far_recv, step_send, step_recv, tail_send, tail_recv, end_send, end_recv, out_send, out_recv,
):
    seq = lax.axis_index("seq")
    tp = lax.axis_index("tp")
    y = lax.rem(seq, 4)
    layer = lax.rem(seq // 4, 2)
    x = seq // 8
    core = lax.rem(tp, 2)
    high = tp // 2
    rows, feats = own_x.shape
    half_rows = rows // 2
    early = feats - LATE
    modes = residue_ref.shape[0]
    step_count = coded.shape[1] // CHUNKS

    def device(x_at, y_at, layer_at, high_at, core_at):
        return ((x_at * 2 + layer_at) * 4 + y_at, high_at * 2 + core_at)

    def wrap(value):
        return lax.rem(value + 2 * RING, RING)

    raw_copy = pltpu.make_async_copy(x_hbm, raw_x, x_sem)
    raw_copy.start()
    w_chunks = raw_w.shape[0]
    w_rows = raw_w.shape[2]
    for chunk in range(w_chunks):
        pltpu.make_async_copy(
            w_hbm.at[:, pl.ds(chunk * w_rows, w_rows), :], raw_w.at[chunk], raw_sem.at[chunk]
        ).start()

    barrier = pltpu.get_barrier_semaphore()
    column = layer * 2 + high * 4 + core

    def greet(target):
        pl.semaphore_signal(barrier, inc=1, device_id=target, device_id_type=MESH)

    for offset in range(1, 8):
        other = lax.rem(column + offset, 8)
        greet(device(x, y, lax.rem(other // 2, 2), other // 4, lax.rem(other, 2)))
    for step in (1, RING - 1):
        greet(device(wrap(x + step), y, layer, high, core))
        greet(device(x, wrap(y + step), layer, high, core))

    raw_copy.wait()
    own_x[...] = raw_x[...].astype(F32).astype(BF16)

    def convert_chunk(chunk):
        pltpu.make_async_copy(
            w_hbm.at[:, pl.ds(chunk * w_rows, w_rows), :], raw_w.at[chunk], raw_sem.at[chunk]
        ).wait()
        for which in range(3):
            for half in range(2):
                place = pl.multiple_of((half ^ high) * (3 * LANES) + which * LANES, LANES)
                both_w[core, pl.ds(pl.multiple_of(chunk * w_rows, w_rows), w_rows), pl.ds(place, LANES)] = (
                    raw_w[chunk, which, :, half * LANES : (half + 1) * LANES].astype(F32).astype(BF16)
                )

    requant = halves_of(high, mult_ref[...].astype(F32) * jnp.exp2(-shift_ref[...].astype(F32)))
    taps = halves_of(high, short_ref[...].astype(F32) * (1.0 / 8192.0))
    rates = halves_of(high, rates_ref[...])
    coeffs = (
        halves_of(high, residue_ref[...].astype(F32))
        * (1.0 / (127.0 * math.sqrt(modes)))
        * jnp.sqrt(small_expm1_neg(2.0 * rates))
    )
    skip = halves_of(high, skip_ref[...])
    decays = jnp.exp(-rates)
    fix_decays = jnp.exp(-rates * float(step_count - 2))
    chunk_decays = jnp.exp(-rates * float(step_count))

    pl.semaphore_wait(barrier, 11)

    home = x * 4 + y

    def by_width(group, action):
        whole = jnp.logical_or(core == layer, jnp.asarray(group == GROUPS - 1))

        @pl.when(whole)
        def _():
            action(feats)

        @pl.when(jnp.logical_not(whole))
        def _():
            action(early)

    def first_copy(part, across):
        at = pl.ds(part * half_rows, half_rows)
        lanes = pl.ds(0, early if across else feats)
        return pltpu.make_async_remote_copy(
            src_ref=own_x.at[at, lanes], dst_ref=all_x.at[home, core, at, lanes],
            send_sem=first_send.at[int(across), part], recv_sem=first_recv.at[core, part],
            device_id=device(x, y, 1 - layer if across else layer, high, layer), device_id_type=MESH,
        )

    for part in range(2):
        first_copy(part, True).start()

        @pl.when(core == layer)
        def _():
            at = pl.ds(part * half_rows, half_rows)
            pltpu.make_async_copy(
                own_x.at[at, :], all_x.at[home, core, at, :], first_recv.at[core, part]
            ).start()

        @pl.when(core != layer)
        def _():
            first_copy(part, False).start()

    sibling = device(x, y, layer, high, 1 - core)

    def w_copy(chunk):
        piece = both_w.at[core, pl.ds(pl.multiple_of(chunk * w_rows, w_rows), w_rows), :]
        return pltpu.make_async_remote_copy(
            src_ref=piece, dst_ref=piece, send_sem=w_send.at[chunk], recv_sem=w_recv.at[chunk],
            device_id=sibling, device_id_type=MESH,
        )

    def w_arrival(chunk):
        piece = both_w.at[1 - core, pl.ds(pl.multiple_of(chunk * w_rows, w_rows), w_rows), :]
        return pltpu.make_async_remote_copy(
            src_ref=piece, dst_ref=piece, send_sem=w_send.at[chunk], recv_sem=w_recv.at[chunk],
            device_id=sibling, device_id_type=MESH,
        )

    def piece_of(axis, group, along):
        shifted = jnp.maximum(group - 1, 0)
        first = jnp.where(group == 0, 1, 0)
        if axis == 0:
            return wrap(x + along) * 4 + wrap(y + shifted), 1 - first
        return wrap(x + shifted) * 4 + wrap(y + along), first

    def part_rows(part):
        return pl.ds(pl.multiple_of(part * half_rows, half_rows), half_rows)

    def ring_copy(axis, way, group, turn, along, feat, width):
        slot, part = piece_of(axis, group, along)
        unit = all_x.at[slot, feat, part_rows(part), pl.ds(0, width)]
        step = 1 if way == 0 else -1
        target = (
            device(wrap(x + step), y, layer, high, core)
            if axis == 0
            else device(x, wrap(y + step), layer, high, core)
        )
        return pltpu.make_async_remote_copy(
            src_ref=unit, dst_ref=unit,
            send_sem=ring_send.at[axis, way, group * 3 + turn],
            recv_sem=ring_recv.at[axis, way, group * 3 + turn],
            device_id=target, device_id_type=MESH,
        )

    def send_own(group, width, axes=(0, 1)):
        for turn in range(2):
            for axis in axes:
                for way in range(2):
                    ring_copy(axis, way, group, turn, 0, turn ^ way, width).start()

    def send_on(group, width):
        for axis in range(2):
            for way in range(2):
                ring_copy(axis, way, group, 2, -1 if way == 0 else 1, way, width).start()

    def wait_own(group, width):
        for turn in range(2):
            for axis in range(2):
                for way in range(2):
                    ring_copy(axis, way, group, turn, -1 if way == 0 else 1, turn ^ way, width).wait_recv()

    def wait_on(group, width):
        for axis in range(2):
            for way in range(2):
                ring_copy(axis, way, group, 2, 2, way, width).wait_recv()

    def late_copies(pieces):
        for slot, part in pieces:
            for feat in range(2):
                place = all_x.at[slot, feat, part_rows(part), pl.ds(early, LATE)]
                number = slot * 4 + part * 2 + feat
                yield pltpu.make_async_remote_copy(
                    src_ref=place, dst_ref=place,
                    send_sem=late_send.at[number], recv_sem=late_recv.at[number],
                    device_id=device(x, y, 1 - layer, high, core), device_id_type=MESH,
                )

    def send_late(pieces):
        @pl.when(core == layer)
        def _():
            for copy in late_copies(pieces):
                copy.start()

    def wait_late(pieces):
        @pl.when(core != layer)
        def _():
            for copy in late_copies(pieces):
                copy.wait_recv()

    far_home = device(x, y, layer, 1 - high, core)

    def far_copies(row):
        piece = row // half_rows
        return (
            pltpu.make_async_remote_copy(
                src_ref=near_codes.at[piece], dst_ref=far_codes.at[piece],
                send_sem=far_send.at[piece], recv_sem=far_recv.at[piece],
                device_id=far_home, device_id_type=MESH,
            ),
            pltpu.make_async_remote_copy(
                src_ref=near_steps.at[piece], dst_ref=far_steps.at[piece],
                send_sem=step_send.at[piece], recv_sem=step_recv.at[piece],
                device_id=far_home, device_id_type=MESH,
            ),
        )

    def multiply(pieces):
        total = None
        for feat in range(2):
            left = jnp.concatenate(
                [
                    all_x[slot, feat, part_rows(part), :]
                    for slot, part in pieces
                ],
                axis=0,
            )
            term = jnp.dot(left, both_w[feat], preferred_element_type=F32)
            total = term if total is None else total + term
        for index, (slot, part) in enumerate(pieces):
            row = pl.multiple_of(slot * rows + part * half_rows, half_rows)
            part_sums = total[index * half_rows : (index + 1) * half_rows]
            sums[pl.ds(row, half_rows), :] = part_sums[:, : 3 * LANES]
            away = part_sums[:, 3 * LANES :]
            peak = jnp.maximum(jnp.max(jnp.abs(away), axis=0, keepdims=True), 1.0)
            near_steps[row // half_rows] = peak * (1.0 / 32767.0)
            scaled = jnp.round(away * (32767.0 / peak))
            near_codes[row // half_rows] = scaled.astype(jnp.int32).astype(jnp.int16)
        for slot, part in pieces:
            for copy in far_copies(slot * rows + part * half_rows):
                copy.start()

    def finish(pieces):
        for slot, part in pieces:
            piece = slot * 2 + part
            for copy in far_copies(piece * half_rows):
                copy.wait_recv()
            at = pl.ds(pl.multiple_of(piece * half_rows, half_rows), half_rows)
            for which in range(3):
                lanes = slice(which * LANES, (which + 1) * LANES)
                away = far_codes[piece, :, lanes].astype(jnp.int32).astype(F32) * far_steps[piece, :, lanes]
                total = (sums[at, lanes] + away) * requant[which : which + 1, :]
                coded[which, at, :] = jnp.clip(total, -127.0, 127.0).astype(BF16).astype(F32)

    def near_pieces(group):
        return [piece_of(axis, group, along) for axis in range(2) for along in (-1, 1)]

    def next_pieces(group):
        return [piece_of(axis, group, 2) for axis in range(2)]

    def second_pieces(group):
        start = group == 0
        return [
            (jnp.where(start, home, slot), jnp.where(start, axis, part))
            for axis, (slot, part) in enumerate(next_pieces(jnp.maximum(group - 1, 0)))
        ]

    def begin_ring(width):
        for part in range(2):
            for feat in range(2):
                landed = all_x.at[home, feat, pl.ds(part * half_rows, half_rows), pl.ds(0, width)]
                pltpu.make_async_copy(landed, landed, first_recv.at[feat, part]).wait()
            send_own(0, width, (part,))
        send_own(1, width)

    @pl.when(core == layer)
    def _():
        begin_ring(feats)

    @pl.loop(0, w_chunks)
    def _(chunk):
        convert_chunk(chunk)
        w_copy(chunk).start()

    @pl.when(core != layer)
    def _():
        begin_ring(early)

    @pl.loop(0, GROUPS)
    def _(group):
        def first_half(width):
            wait_own(group, width)
            send_on(group, width)

        by_width(group, first_half)
        near = near_pieces(group)

        @pl.when(group < GROUPS - 1)
        def _():
            send_late(near)

        @pl.when(group == 0)
        def _():
            @pl.loop(0, w_chunks)
            def _(chunk):
                w_arrival(chunk).wait_recv()

        @pl.when(group < GROUPS - 1)
        def _():
            wait_late(near)

        multiply(near)

        @pl.when(group > 0)
        def _():
            finish(near_pieces(group - 1))

        @pl.when(group > 0)
        def _():
            by_width(group - 1, lambda width: wait_on(group - 1, width))

        @pl.when(group + 2 < GROUPS)
        def _():
            by_width(group + 2, lambda width: send_own(group + 2, width))

        second = second_pieces(group)
        send_late(second)
        wait_late(second)
        multiply(second)

        @pl.when(group > 0)
        def _():
            finish(second_pieces(group - 1))

    finish(near_pieces(GROUPS - 1))

    for part in range(2):
        first_copy(part, True).wait_send()

        @pl.when(core != layer)
        def _():
            first_copy(part, False).wait_send()

    @pl.loop(0, w_chunks)
    def _(chunk):
        w_copy(chunk).wait_send()

    def sent_turn(group, turn, width):
        for axis in range(2):
            for way in range(2):
                ring_copy(axis, way, group, turn, 0, 0, width).wait_send()

    @pl.loop(0, GROUPS)
    def _(group):
        def sent_own(width):
            for turn in range(2):
                sent_turn(group, turn, width)

        by_width(group, sent_own)

    @pl.loop(0, GROUPS - 1)
    def _(group):
        by_width(group, lambda width: sent_turn(group, 2, width))

    @pl.when(core == layer)
    def _():
        for copy in late_copies([(home, 0), (home, 1)]):
            copy.wait_send()

        @pl.loop(0, GROUPS - 1)
        def _(group):
            for copy in late_copies(near_pieces(group) + next_pieces(group)):
                copy.wait_send()

    by_width(GROUPS - 1, lambda width: wait_on(GROUPS - 1, width))
    last = next_pieces(GROUPS - 1)
    multiply(last)
    finish(second_pieces(GROUPS - 1))
    by_width(GROUPS - 1, lambda width: sent_turn(GROUPS - 1, 2, width))

    @pl.loop(0, near_codes.shape[0])
    def _(piece):
        for copy in far_copies(piece * half_rows):
            copy.wait_send()

    finish(last)

    for back in range(2):
        for which in range(3):
            tails[back, which] = coded[which, pl.ds(step_count - 1 - back, CHUNKS, stride=step_count), :]
    tail_copy = pltpu.make_async_remote_copy(
        src_ref=tails, dst_ref=sib_tails, send_sem=tail_send, recv_sem=tail_recv,
        device_id=sibling, device_id_type=MESH,
    )
    tail_copy.start()

    def spread(row):
        return jnp.broadcast_to(row, (CHUNKS, LANES))

    tap_rows = [[spread(taps[lag, which : which + 1, :]) for which in range(3)] for lag in range(3)]
    decay_rows = [spread(decays[mode : mode + 1, :]) for mode in range(modes)]
    index = lax.broadcasted_iota(jnp.int32, (CHUNKS, LANES), 0)
    odd = lax.rem(index, 2) == 1

    def before_chunk(back, which):
        own = pltpu.roll(tails[back, which], 1, 0)
        other = sib_tails[back, which]
        up = pltpu.roll(other, 1, 0)
        down = pltpu.roll(other, CHUNKS - 1, 0)
        outside = jnp.where(core == 0, jnp.where(index == 0, 0.0, up), down)
        return jnp.where(odd, own, outside)

    half_modes = modes // 2

    def load_step(step):
        return tuple(coded[which, pl.ds(step, CHUNKS, stride=step_count), :] for which in range(3))

    def featurize(step, now, newer, older):
        feat = [
            tap_rows[0][which] * now[which]
            + tap_rows[1][which] * newer[which]
            + tap_rows[2][which] * older[which]
            for which in range(3)
        ]
        drive = feat[1] * feat[2]
        at = pl.ds(pl.multiple_of(step * CHUNKS, CHUNKS), CHUNKS)
        queries[at, :] = feat[0]
        drives[at, :] = drive
        return drive

    def advance(states, drive, half):
        return tuple(
            decay_rows[half * half_modes + mode] * states[mode] + drive for mode in range(half_modes)
        )

    def first_pass(step, carry):
        older, newer, states = carry
        now = load_step(step)
        drive = featurize(step, now, newer, older)
        return newer, now, advance(states, drive, 0)

    def load_drive(step):
        return drives[pl.ds(pl.multiple_of(step * CHUNKS, CHUNKS), CHUNKS), :]

    def send_ends(half, states):
        for mode in range(half_modes):
            ends[half, mode * CHUNKS : (mode + 1) * CHUNKS, :] = states[mode]
        end_copy(half).start()

    def end_copy(half):
        return pltpu.make_async_remote_copy(
            src_ref=ends.at[half], dst_ref=sib_ends.at[half],
            send_sem=end_send.at[half], recv_sem=end_recv.at[half],
            device_id=sibling, device_id_type=MESH,
        )

    def start_states(half):
        end_copy(half).wait_recv()
        state = jnp.zeros((half_modes, LANES), F32)
        ratio = chunk_decays[half * half_modes : (half + 1) * half_modes, :]
        for run in range(CHUNKS // 2):
            for owner in range(2):
                for chunk in (2 * run, 2 * run + 1):
                    rows_at = pl.ds(chunk, half_modes, stride=CHUNKS)
                    starts[owner, rows_at, :] = state
                    ended = jnp.where(core == owner, ends[half, rows_at, :], sib_ends[half, rows_at, :])
                    state = ratio * state + ended
        return tuple(starts[core, mode * CHUNKS : (mode + 1) * CHUNKS, :] for mode in range(half_modes))

    zeros = tuple(jnp.zeros((CHUNKS, LANES), F32) for _ in range(half_modes))
    step_0, step_1 = load_step(0), load_step(1)
    _, _, states = lax.fori_loop(2, step_count, first_pass, (step_0, step_1, zeros), unroll=2)
    tail_copy.wait_recv()
    back_1 = tuple(before_chunk(0, which) for which in range(3))
    back_2 = tuple(before_chunk(1, which) for which in range(3))
    drive_0 = featurize(0, step_0, back_1, back_2)
    drive_1 = featurize(1, step_1, step_0, back_1)
    states = tuple(
        states[mode] + spread(fix_decays[mode : mode + 1, :]) * (decay_rows[mode] * drive_0 + drive_1)
        for mode in range(half_modes)
    )
    send_ends(0, states)
    states = lax.fori_loop(
        0, step_count, lambda step, held: advance(held, load_drive(step), 1), zeros, unroll=4
    )
    send_ends(1, states)
    coeff_rows = [spread(coeffs[mode : mode + 1, :]) for mode in range(modes)]
    skip_row = spread(skip)

    def weigh(states, half):
        parts = [coeff_rows[half * half_modes + mode] * states[mode] for mode in range(half_modes)]
        while len(parts) > 1:
            parts = [parts[i] + parts[i + 1] for i in range(0, len(parts), 2)]
        return parts[0]

    def middle_pass(step, states):
        at = pl.ds(pl.multiple_of(step * CHUNKS, CHUNKS), CHUNKS)
        drive = drives[at, :]
        states = advance(states, drive, 0)
        gated[at, :] = weigh(states, 0) + skip_row * drive
        return states

    lax.fori_loop(0, step_count, middle_pass, start_states(0), unroll=4)

    out_rows = out_ref.shape[0]
    blocks = step_count // out_rows
    channel = pl.multiple_of((seq * 2 + high) * LANES, LANES)

    def second_pass(step, states):
        at = pl.ds(pl.multiple_of(step * CHUNKS, CHUNKS), CHUNKS)
        states = advance(states, drives[at, :], 1)
        gated[at, :] = queries[at, :] * (gated[at, :] + weigh(states, 1))
        return states

    place = out_ref.at[:, pl.ds(channel, LANES)]
    first_seat = core * 4

    def send_outs(block):
        row = first_seat + block // 4
        tp_at = lax.rem(block, 4)
        for chunk in range(CHUNKS):
            seq_at = row + (chunk // 2) * 8 + (chunk % 2) * 2
            is_me = jnp.logical_and(seq_at == seq, tp_at == tp)

            @pl.when(is_me)
            def _():
                pltpu.make_async_copy(staged.at[block, chunk], place, out_recv).start()

            @pl.when(jnp.logical_not(is_me))
            def _():
                pltpu.make_async_remote_copy(
                    src_ref=staged.at[block, chunk], dst_ref=place, send_sem=out_send, recv_sem=out_recv,
                    device_id=(seq_at, tp_at), device_id_type=MESH,
                ).start()

    def out_block(block, states):
        states = lax.fori_loop(
            0, out_rows, lambda step, held: second_pass(block * out_rows + step, held), states, unroll=4
        )
        for chunk in range(CHUNKS):
            taken = gated[pl.ds(block * (out_rows * CHUNKS) + chunk, out_rows, stride=CHUNKS), :]
            staged[block, chunk] = taken.astype(BF16)
        send_outs(block)
        return states

    lax.fori_loop(0, blocks, out_block, start_states(1))

    tail_copy.wait_send()
    for half in range(2):
        end_copy(half).wait_send()
    pltpu.make_async_copy(out_ref, out_ref, out_recv).wait()
    sent = staged.at[pl.ds(1, blocks - 1)]
    pltpu.make_async_copy(sent, sent, out_send).wait()
    most = staged.at[0, pl.ds(1, CHUNKS - 1)]
    pltpu.make_async_copy(most, most, out_send).wait()

    @pl.when(core != layer)
    def _():
        pltpu.make_async_copy(staged.at[0, 0], staged.at[0, 0], out_send).wait()


def on_device(x_codes, w_codes, req_mult, req_shift, short_codes, residue_codes, rates, skip_gain):
    rows, feats = x_codes.shape
    seq_devs = lax.axis_size("seq")
    tp_devs = lax.axis_size("tp")
    cols = w_codes.shape[2]
    positions = rows * seq_devs // 2
    modes = residue_codes.shape[0]
    out_rows = rows // tp_devs
    steps = positions // CHUNKS
    blocks = steps // out_rows
    pieces = 2 * positions // rows
    w_rows = 256
    w_chunks = feats // w_rows
    vmem = pl.BlockSpec(memory_space=pltpu.VMEM)
    dma = pltpu.SemaphoreType.DMA
    return pl.pallas_call(
        hyena_kernel,
        out_shape=jax.ShapeDtypeStruct((out_rows, cols * seq_devs), BF16),
        in_specs=[pl.BlockSpec(memory_space=pl.ANY)] * 2 + [vmem] * 6,
        out_specs=pl.BlockSpec(memory_space=pl.ANY),
        scratch_shapes=[
            pltpu.VMEM((rows, feats), jnp.int32),
            pltpu.VMEM((rows, feats), BF16),
            pltpu.VMEM((seq_devs // 2, 2, rows, feats), BF16),
            pltpu.VMEM((w_chunks, 3, w_rows, cols), jnp.int32),
            pltpu.VMEM((2, feats, 3 * cols), BF16),
            pltpu.VMEM((positions, 3 * LANES), F32),
            pltpu.VMEM((pieces, rows // 2, 3 * LANES), jnp.int16),
            pltpu.VMEM((pieces, 1, 3 * LANES), F32),
            pltpu.VMEM((pieces, rows // 2, 3 * LANES), jnp.int16),
            pltpu.VMEM((pieces, 1, 3 * LANES), F32),
            pltpu.VMEM((3, positions, LANES), F32),
            pltpu.VMEM((2, 3, CHUNKS, LANES), F32),
            pltpu.VMEM((2, 3, CHUNKS, LANES), F32),
            pltpu.VMEM((2, modes // 2 * CHUNKS, LANES), F32),
            pltpu.VMEM((2, modes // 2 * CHUNKS, LANES), F32),
            pltpu.VMEM((2, modes // 2 * CHUNKS, LANES), F32),
            pltpu.VMEM((positions, LANES), F32),
            pltpu.VMEM((positions, LANES), F32),
            pltpu.VMEM((positions, LANES), F32),
            pltpu.VMEM((blocks, CHUNKS, out_rows, LANES), BF16),
            dma,
            dma((2, 2)),
            dma((2, 2)),
            dma((w_chunks,)),
            dma((w_chunks,)),
            dma((w_chunks,)),
            dma((2, 2, 3 * GROUPS)),
            dma((2, 2, 3 * GROUPS)),
            dma((2 * pieces,)),
            dma((2 * pieces,)),
            dma((pieces,)),
            dma((pieces,)),
            dma((pieces,)),
            dma((pieces,)),
            dma,
            dma,
            dma((2,)),
            dma((2,)),
            dma,
            dma,
        ],
        compiler_params=pltpu.CompilerParams(
            collective_id=0, has_side_effects=True, vmem_limit_bytes=64 * 1024 * 1024 - 65536
        ),
    )(x_codes, w_codes, req_mult, req_shift, short_codes, residue_codes, rates, skip_gain.reshape(1, -1))


def solution(mesh):
    placed = (
        P("seq", "tp"),
        P(None, "tp", "seq"),
        P(None, "seq"),
        P(None, "seq"),
        P(None, None, "seq"),
        P(None, "seq"),
        P(None, "seq"),
        P("seq"),
    )
    return jax.shard_map(
        on_device, mesh=mesh, in_specs=placed, out_specs=P(("seq", "tp"), None), check_vma=False
    )
```

```python
import functools
import math

import jax
import jax.numpy as jnp
from jax import lax
from jax.experimental import pallas as pl
from jax.experimental.pallas import tpu as pltpu
from jax.sharding import PartitionSpec as P

MESH = pl.DeviceIdType.MESH
F32 = jnp.float32
BF16 = jnp.bfloat16
LANES = 128
CHUNKS = 8
RING = 4
GROUPS = 5
LATE = 512
WHOLE_FROM = 3


def halves_of(which, array):
    return jnp.where(which == 0, array[..., :LANES], array[..., LANES:])


def small_expm1_neg(z):
    poly = jnp.ones_like(z)
    for order in range(8, 1, -1):
        poly = 1.0 - (z * (1.0 / order)) * poly
    return z * poly


def hyena_kernel(
    x_hbm, w_hbm, mult_ref, shift_ref, short_ref, residue_ref, rates_ref, skip_ref,
    out_ref,
    raw_x, own_x, all_x, raw_w, both_w, sums, near_codes, near_steps, far_codes, far_steps, coded, tails, sib_tails, ends, sib_ends,
    starts, queries, drives, gated, staged,
    x_sem, first_send, first_recv, raw_sem, w_send, w_recv, ring_send, ring_recv, late_send, late_recv,
    far_send, far_recv, step_send, step_recv, tail_send, tail_recv, end_send, end_recv, out_send, out_recv,
):
    seq = lax.axis_index("seq")
    tp = lax.axis_index("tp")
    y = lax.rem(seq, 4)
    layer = lax.rem(seq // 4, 2)
    x = seq // 8
    core = lax.rem(tp, 2)
    high = tp // 2
    rows, feats = own_x.shape
    half_rows = rows // 2
    early = feats - LATE
    modes = residue_ref.shape[0]
    step_count = coded.shape[1] // CHUNKS

    def device(x_at, y_at, layer_at, high_at, core_at):
        return ((x_at * 2 + layer_at) * 4 + y_at, high_at * 2 + core_at)

    def wrap(value):
        return lax.rem(value + 2 * RING, RING)

    raw_copy = pltpu.make_async_copy(x_hbm, raw_x, x_sem)
    raw_copy.start()
    w_chunks = raw_w.shape[0]
    w_rows = raw_w.shape[2]
    for chunk in range(w_chunks):
        pltpu.make_async_copy(
            w_hbm.at[:, pl.ds(chunk * w_rows, w_rows), :], raw_w.at[chunk], raw_sem.at[chunk]
        ).start()

    barrier = pltpu.get_barrier_semaphore()
    column = layer * 2 + high * 4 + core

    def greet(target):
        pl.semaphore_signal(barrier, inc=1, device_id=target, device_id_type=MESH)

    for offset in range(1, 8):
        other = lax.rem(column + offset, 8)
        greet(device(x, y, lax.rem(other // 2, 2), other // 4, lax.rem(other, 2)))
    for step in (1, RING - 1):
        greet(device(wrap(x + step), y, layer, high, core))
        greet(device(x, wrap(y + step), layer, high, core))

    raw_copy.wait()
    own_x[...] = raw_x[...].astype(F32).astype(BF16)

    def convert_chunk(chunk):
        pltpu.make_async_copy(
            w_hbm.at[:, pl.ds(chunk * w_rows, w_rows), :], raw_w.at[chunk], raw_sem.at[chunk]
        ).wait()
        for which in range(3):
            for half in range(2):
                place = pl.multiple_of((half ^ high) * (3 * LANES) + which * LANES, LANES)
                both_w[core, pl.ds(pl.multiple_of(chunk * w_rows, w_rows), w_rows), pl.ds(place, LANES)] = (
                    raw_w[chunk, which, :, half * LANES : (half + 1) * LANES].astype(F32).astype(BF16)
                )

    requant = halves_of(high, mult_ref[...].astype(F32) * jnp.exp2(-shift_ref[...].astype(F32)))
    taps = halves_of(high, short_ref[...].astype(F32) * (1.0 / 8192.0))
    rates = halves_of(high, rates_ref[...])
    coeffs = (
        halves_of(high, residue_ref[...].astype(F32))
        * (1.0 / (127.0 * math.sqrt(modes)))
        * jnp.sqrt(small_expm1_neg(2.0 * rates))
    )
    skip = halves_of(high, skip_ref[...])
    decays = jnp.exp(-rates)
    fix_decays = jnp.exp(-rates * float(step_count - 2))
    chunk_decays = jnp.exp(-rates * float(step_count))

    pl.semaphore_wait(barrier, 11)

    home = x * 4 + y

    def by_width(group, action):
        whole = jnp.logical_or(core == layer, jnp.asarray(group >= WHOLE_FROM))

        @pl.when(whole)
        def _():
            action(feats)

        @pl.when(jnp.logical_not(whole))
        def _():
            action(early)

    def first_copy(part, across):
        at = pl.ds(part * half_rows, half_rows)
        lanes = pl.ds(0, early if across else feats)
        return pltpu.make_async_remote_copy(
            src_ref=own_x.at[at, lanes], dst_ref=all_x.at[home, core, at, lanes],
            send_sem=first_send.at[int(across), part], recv_sem=first_recv.at[core, part],
            device_id=device(x, y, 1 - layer if across else layer, high, layer), device_id_type=MESH,
        )

    for part in range(2):
        first_copy(part, True).start()

        @pl.when(core == layer)
        def _():
            at = pl.ds(part * half_rows, half_rows)
            pltpu.make_async_copy(
                own_x.at[at, :], all_x.at[home, core, at, :], first_recv.at[core, part]
            ).start()

        @pl.when(core != layer)
        def _():
            first_copy(part, False).start()

    sibling = device(x, y, layer, high, 1 - core)

    def w_copy(chunk):
        piece = both_w.at[core, pl.ds(pl.multiple_of(chunk * w_rows, w_rows), w_rows), :]
        return pltpu.make_async_remote_copy(
            src_ref=piece, dst_ref=piece, send_sem=w_send.at[chunk], recv_sem=w_recv.at[chunk],
            device_id=sibling, device_id_type=MESH,
        )

    def w_arrival(chunk):
        piece = both_w.at[1 - core, pl.ds(pl.multiple_of(chunk * w_rows, w_rows), w_rows), :]
        return pltpu.make_async_remote_copy(
            src_ref=piece, dst_ref=piece, send_sem=w_send.at[chunk], recv_sem=w_recv.at[chunk],
            device_id=sibling, device_id_type=MESH,
        )

    def piece_of(axis, group, along):
        shifted = jnp.maximum(group - 1, 0)
        first = jnp.where(group == 0, 1, 0)
        if axis == 0:
            return wrap(x + along) * 4 + wrap(y + shifted), 1 - first
        return wrap(x + shifted) * 4 + wrap(y + along), first

    def part_rows(part):
        return pl.ds(pl.multiple_of(part * half_rows, half_rows), half_rows)

    def ring_copy(axis, way, group, turn, along, feat, width):
        slot, part = piece_of(axis, group, along)
        unit = all_x.at[slot, feat, part_rows(part), pl.ds(0, width)]
        step = 1 if way == 0 else -1
        target = (
            device(wrap(x + step), y, layer, high, core)
            if axis == 0
            else device(x, wrap(y + step), layer, high, core)
        )
        return pltpu.make_async_remote_copy(
            src_ref=unit, dst_ref=unit,
            send_sem=ring_send.at[axis, way, group * 3 + turn],
            recv_sem=ring_recv.at[axis, way, group * 3 + turn],
            device_id=target, device_id_type=MESH,
        )

    def send_own(group, width, axes=(0, 1)):
        for turn in range(2):
            for axis in axes:
                for way in range(2):
                    ring_copy(axis, way, group, turn, 0, turn ^ way, width).start()

    def send_on(group, width):
        for axis in range(2):
            for way in range(2):
                ring_copy(axis, way, group, 2, -1 if way == 0 else 1, way, width).start()

    def wait_own(group, width):
        for turn in range(2):
            for axis in range(2):
                for way in range(2):
                    ring_copy(axis, way, group, turn, -1 if way == 0 else 1, turn ^ way, width).wait_recv()

    def wait_on(group, width):
        for axis in range(2):
            for way in range(2):
                ring_copy(axis, way, group, 2, 2, way, width).wait_recv()

    def late_copies(pieces):
        for slot, part in pieces:
            for feat in range(2):
                place = all_x.at[slot, feat, part_rows(part), pl.ds(early, LATE)]
                number = slot * 4 + part * 2 + feat
                yield pltpu.make_async_remote_copy(
                    src_ref=place, dst_ref=place,
                    send_sem=late_send.at[number], recv_sem=late_recv.at[number],
                    device_id=device(x, y, 1 - layer, high, core), device_id_type=MESH,
                )

    def send_late(pieces):
        @pl.when(core == layer)
        def _():
            for copy in late_copies(pieces):
                copy.start()

    def wait_late(pieces):
        @pl.when(core != layer)
        def _():
            for copy in late_copies(pieces):
                copy.wait_recv()

    far_home = device(x, y, layer, 1 - high, core)

    def far_copies(row):
        piece = row // half_rows
        return (
            pltpu.make_async_remote_copy(
                src_ref=near_codes.at[piece], dst_ref=far_codes.at[piece],
                send_sem=far_send.at[piece], recv_sem=far_recv.at[piece],
                device_id=far_home, device_id_type=MESH,
            ),
            pltpu.make_async_remote_copy(
                src_ref=near_steps.at[piece], dst_ref=far_steps.at[piece],
                send_sem=step_send.at[piece], recv_sem=step_recv.at[piece],
                device_id=far_home, device_id_type=MESH,
            ),
        )

    def multiply(pieces):
        total = None
        for feat in range(2):
            left = jnp.concatenate(
                [
                    all_x[slot, feat, part_rows(part), :]
                    for slot, part in pieces
                ],
                axis=0,
            )
            term = jnp.dot(left, both_w[feat], preferred_element_type=F32)
            total = term if total is None else total + term
        for index, (slot, part) in enumerate(pieces):
            row = pl.multiple_of(slot * rows + part * half_rows, half_rows)
            part_sums = total[index * half_rows : (index + 1) * half_rows]
            sums[pl.ds(row, half_rows), :] = part_sums[:, : 3 * LANES]
            away = part_sums[:, 3 * LANES :]
            peak = jnp.maximum(jnp.max(jnp.abs(away), axis=0, keepdims=True), 1.0)
            near_steps[row // half_rows] = peak * (1.0 / 32767.0)
            scaled = jnp.round(away * (32767.0 / peak))
            near_codes[row // half_rows] = scaled.astype(jnp.int32).astype(jnp.int16)
        for slot, part in pieces:
            for copy in far_copies(slot * rows + part * half_rows):
                copy.start()

    def finish(pieces):
        for slot, part in pieces:
            piece = slot * 2 + part
            for copy in far_copies(piece * half_rows):
                copy.wait_recv()
            at = pl.ds(pl.multiple_of(piece * half_rows, half_rows), half_rows)
            for which in range(3):
                lanes = slice(which * LANES, (which + 1) * LANES)
                away = far_codes[piece, :, lanes].astype(jnp.int32).astype(F32) * far_steps[piece, :, lanes]
                total = (sums[at, lanes] + away) * requant[which : which + 1, :]
                coded[which, at, :] = jnp.clip(total, -127.0, 127.0).astype(BF16).astype(F32)

    def near_pieces(group):
        return [piece_of(axis, group, along) for axis in range(2) for along in (-1, 1)]

    def next_pieces(group):
        return [piece_of(axis, group, 2) for axis in range(2)]

    def second_pieces(group):
        start = group == 0
        return [
            (jnp.where(start, home, slot), jnp.where(start, axis, part))
            for axis, (slot, part) in enumerate(next_pieces(jnp.maximum(group - 1, 0)))
        ]

    def begin_ring(width):
        for part in range(2):
            for feat in range(2):
                landed = all_x.at[home, feat, pl.ds(part * half_rows, half_rows), pl.ds(0, width)]
                pltpu.make_async_copy(landed, landed, first_recv.at[feat, part]).wait()
            send_own(0, width, (part,))
        send_own(1, width)

    @pl.when(core == layer)
    def _():
        begin_ring(feats)

    @pl.loop(0, w_chunks)
    def _(chunk):
        convert_chunk(chunk)
        w_copy(chunk).start()

    @pl.when(core != layer)
    def _():
        begin_ring(early)

    @pl.loop(0, GROUPS)
    def _(group):
        def first_half(width):
            wait_own(group, width)
            send_on(group, width)

        by_width(group, first_half)
        near = near_pieces(group)

        @pl.when(group < WHOLE_FROM)
        def _():
            send_late(near)

        @pl.when(group == 0)
        def _():
            @pl.loop(0, w_chunks)
            def _(chunk):
                w_arrival(chunk).wait_recv()

        @pl.when(group < WHOLE_FROM)
        def _():
            wait_late(near)

        multiply(near)

        @pl.when(group > 0)
        def _():
            finish(near_pieces(group - 1))

        @pl.when(group > 0)
        def _():
            by_width(group - 1, lambda width: wait_on(group - 1, width))

        second = second_pieces(group)

        @pl.when(group <= WHOLE_FROM)
        def _():
            send_late(second)
            wait_late(second)

        @pl.when(group + 2 < GROUPS)
        def _():
            by_width(group + 2, lambda width: send_own(group + 2, width))

        multiply(second)

        @pl.when(group > 0)
        def _():
            finish(second_pieces(group - 1))

    finish(near_pieces(GROUPS - 1))

    for part in range(2):
        first_copy(part, True).wait_send()

        @pl.when(core != layer)
        def _():
            first_copy(part, False).wait_send()

    @pl.loop(0, w_chunks)
    def _(chunk):
        w_copy(chunk).wait_send()

    def sent_turn(group, turn, width):
        for axis in range(2):
            for way in range(2):
                ring_copy(axis, way, group, turn, 0, 0, width).wait_send()

    @pl.loop(0, GROUPS)
    def _(group):
        def sent_own(width):
            for turn in range(2):
                sent_turn(group, turn, width)

        by_width(group, sent_own)

    @pl.loop(0, GROUPS - 1)
    def _(group):
        by_width(group, lambda width: sent_turn(group, 2, width))

    @pl.when(core == layer)
    def _():
        for copy in late_copies([(home, 0), (home, 1)]):
            copy.wait_send()

        @pl.loop(0, WHOLE_FROM)
        def _(group):
            for copy in late_copies(near_pieces(group) + next_pieces(group)):
                copy.wait_send()

    by_width(GROUPS - 1, lambda width: wait_on(GROUPS - 1, width))
    last = next_pieces(GROUPS - 1)
    multiply(last)
    finish(second_pieces(GROUPS - 1))
    by_width(GROUPS - 1, lambda width: sent_turn(GROUPS - 1, 2, width))

    @pl.loop(0, near_codes.shape[0])
    def _(piece):
        for copy in far_copies(piece * half_rows):
            copy.wait_send()

    finish(last)

    for back in range(2):
        for which in range(3):
            tails[back, which] = coded[which, pl.ds(step_count - 1 - back, CHUNKS, stride=step_count), :]
    tail_copy = pltpu.make_async_remote_copy(
        src_ref=tails, dst_ref=sib_tails, send_sem=tail_send, recv_sem=tail_recv,
        device_id=sibling, device_id_type=MESH,
    )
    tail_copy.start()

    def spread(row):
        return jnp.broadcast_to(row, (CHUNKS, LANES))

    tap_rows = [[spread(taps[lag, which : which + 1, :]) for which in range(3)] for lag in range(3)]
    decay_rows = [spread(decays[mode : mode + 1, :]) for mode in range(modes)]
    index = lax.broadcasted_iota(jnp.int32, (CHUNKS, LANES), 0)
    odd = lax.rem(index, 2) == 1

    def before_chunk(back, which):
        own = pltpu.roll(tails[back, which], 1, 0)
        other = sib_tails[back, which]
        up = pltpu.roll(other, 1, 0)
        down = pltpu.roll(other, CHUNKS - 1, 0)
        outside = jnp.where(core == 0, jnp.where(index == 0, 0.0, up), down)
        return jnp.where(odd, own, outside)

    half_modes = modes // 2

    def load_step(step):
        return tuple(coded[which, pl.ds(step, CHUNKS, stride=step_count), :] for which in range(3))

    def featurize(step, now, newer, older):
        feat = [
            tap_rows[0][which] * now[which]
            + tap_rows[1][which] * newer[which]
            + tap_rows[2][which] * older[which]
            for which in range(3)
        ]
        drive = feat[1] * feat[2]
        at = pl.ds(pl.multiple_of(step * CHUNKS, CHUNKS), CHUNKS)
        queries[at, :] = feat[0]
        drives[at, :] = drive
        return drive

    def advance(states, drive, half):
        return tuple(
            decay_rows[half * half_modes + mode] * states[mode] + drive for mode in range(half_modes)
        )

    def first_pass(step, carry):
        older, newer, states = carry
        now = load_step(step)
        drive = featurize(step, now, newer, older)
        return newer, now, advance(states, drive, 0)

    def load_drive(step):
        return drives[pl.ds(pl.multiple_of(step * CHUNKS, CHUNKS), CHUNKS), :]

    def send_ends(half, states):
        for mode in range(half_modes):
            ends[half, mode * CHUNKS : (mode + 1) * CHUNKS, :] = states[mode]
        end_copy(half).start()

    def end_copy(half):
        return pltpu.make_async_remote_copy(
            src_ref=ends.at[half], dst_ref=sib_ends.at[half],
            send_sem=end_send.at[half], recv_sem=end_recv.at[half],
            device_id=sibling, device_id_type=MESH,
        )

    def start_states(half):
        end_copy(half).wait_recv()
        state = jnp.zeros((half_modes, LANES), F32)
        ratio = chunk_decays[half * half_modes : (half + 1) * half_modes, :]
        for run in range(CHUNKS // 2):
            for owner in range(2):
                for chunk in (2 * run, 2 * run + 1):
                    rows_at = pl.ds(chunk, half_modes, stride=CHUNKS)
                    starts[owner, rows_at, :] = state
                    ended = jnp.where(core == owner, ends[half, rows_at, :], sib_ends[half, rows_at, :])
                    state = ratio * state + ended
        return tuple(starts[core, mode * CHUNKS : (mode + 1) * CHUNKS, :] for mode in range(half_modes))

    zeros = tuple(jnp.zeros((CHUNKS, LANES), F32) for _ in range(half_modes))
    step_0, step_1 = load_step(0), load_step(1)
    _, _, states = lax.fori_loop(2, step_count, first_pass, (step_0, step_1, zeros), unroll=2)
    tail_copy.wait_recv()
    back_1 = tuple(before_chunk(0, which) for which in range(3))
    back_2 = tuple(before_chunk(1, which) for which in range(3))
    drive_0 = featurize(0, step_0, back_1, back_2)
    drive_1 = featurize(1, step_1, step_0, back_1)
    states = tuple(
        states[mode] + spread(fix_decays[mode : mode + 1, :]) * (decay_rows[mode] * drive_0 + drive_1)
        for mode in range(half_modes)
    )
    send_ends(0, states)
    states = lax.fori_loop(
        0, step_count, lambda step, held: advance(held, load_drive(step), 1), zeros, unroll=4
    )
    send_ends(1, states)
    coeff_rows = [spread(coeffs[mode : mode + 1, :]) for mode in range(modes)]
    skip_row = spread(skip)

    def weigh(states, half):
        parts = [coeff_rows[half * half_modes + mode] * states[mode] for mode in range(half_modes)]
        while len(parts) > 1:
            parts = [parts[i] + parts[i + 1] for i in range(0, len(parts), 2)]
        return parts[0]

    def middle_pass(step, states):
        at = pl.ds(pl.multiple_of(step * CHUNKS, CHUNKS), CHUNKS)
        drive = drives[at, :]
        states = advance(states, drive, 0)
        gated[at, :] = weigh(states, 0) + skip_row * drive
        return states

    lax.fori_loop(0, step_count, middle_pass, start_states(0), unroll=4)

    out_rows = out_ref.shape[0]
    blocks = step_count // out_rows
    channel = pl.multiple_of((seq * 2 + high) * LANES, LANES)

    def second_pass(step, states):
        at = pl.ds(pl.multiple_of(step * CHUNKS, CHUNKS), CHUNKS)
        states = advance(states, drives[at, :], 1)
        gated[at, :] = queries[at, :] * (gated[at, :] + weigh(states, 1))
        return states

    place = out_ref.at[:, pl.ds(channel, LANES)]
    first_seat = core * 4

    def send_outs(block):
        row = first_seat + block // 4
        tp_at = lax.rem(block, 4)
        for chunk in range(CHUNKS):
            seq_at = row + (chunk // 2) * 8 + (chunk % 2) * 2
            is_me = jnp.logical_and(seq_at == seq, tp_at == tp)

            @pl.when(is_me)
            def _():
                pltpu.make_async_copy(staged.at[block, chunk], place, out_recv).start()

            @pl.when(jnp.logical_not(is_me))
            def _():
                pltpu.make_async_remote_copy(
                    src_ref=staged.at[block, chunk], dst_ref=place, send_sem=out_send, recv_sem=out_recv,
                    device_id=(seq_at, tp_at), device_id_type=MESH,
                ).start()

    def out_block(block, states):
        states = lax.fori_loop(
            0, out_rows, lambda step, held: second_pass(block * out_rows + step, held), states, unroll=4
        )
        for chunk in range(CHUNKS):
            taken = gated[pl.ds(block * (out_rows * CHUNKS) + chunk, out_rows, stride=CHUNKS), :]
            staged[block, chunk] = taken.astype(BF16)
        send_outs(block)
        return states

    lax.fori_loop(0, blocks, out_block, start_states(1))

    tail_copy.wait_send()
    for half in range(2):
        end_copy(half).wait_send()
    pltpu.make_async_copy(out_ref, out_ref, out_recv).wait()
    sent = staged.at[pl.ds(1, blocks - 1)]
    pltpu.make_async_copy(sent, sent, out_send).wait()
    most = staged.at[0, pl.ds(1, CHUNKS - 1)]
    pltpu.make_async_copy(most, most, out_send).wait()

    @pl.when(core != layer)
    def _():
        pltpu.make_async_copy(staged.at[0, 0], staged.at[0, 0], out_send).wait()


def on_device(x_codes, w_codes, req_mult, req_shift, short_codes, residue_codes, rates, skip_gain):
    rows, feats = x_codes.shape
    seq_devs = lax.axis_size("seq")
    tp_devs = lax.axis_size("tp")
    cols = w_codes.shape[2]
    positions = rows * seq_devs // 2
    modes = residue_codes.shape[0]
    out_rows = rows // tp_devs
    steps = positions // CHUNKS
    blocks = steps // out_rows
    pieces = 2 * positions // rows
    w_rows = 256
    w_chunks = feats // w_rows
    vmem = pl.BlockSpec(memory_space=pltpu.VMEM)
    dma = pltpu.SemaphoreType.DMA
    return pl.pallas_call(
        hyena_kernel,
        out_shape=jax.ShapeDtypeStruct((out_rows, cols * seq_devs), BF16),
        in_specs=[pl.BlockSpec(memory_space=pl.ANY)] * 2 + [vmem] * 6,
        out_specs=pl.BlockSpec(memory_space=pl.ANY),
        scratch_shapes=[
            pltpu.VMEM((rows, feats), jnp.int32),
            pltpu.VMEM((rows, feats), BF16),
            pltpu.VMEM((seq_devs // 2, 2, rows, feats), BF16),
            pltpu.VMEM((w_chunks, 3, w_rows, cols), jnp.int32),
            pltpu.VMEM((2, feats, 3 * cols), BF16),
            pltpu.VMEM((positions, 3 * LANES), F32),
            pltpu.VMEM((pieces, rows // 2, 3 * LANES), jnp.int16),
            pltpu.VMEM((pieces, 1, 3 * LANES), F32),
            pltpu.VMEM((pieces, rows // 2, 3 * LANES), jnp.int16),
            pltpu.VMEM((pieces, 1, 3 * LANES), F32),
            pltpu.VMEM((3, positions, LANES), F32),
            pltpu.VMEM((2, 3, CHUNKS, LANES), F32),
            pltpu.VMEM((2, 3, CHUNKS, LANES), F32),
            pltpu.VMEM((2, modes // 2 * CHUNKS, LANES), F32),
            pltpu.VMEM((2, modes // 2 * CHUNKS, LANES), F32),
            pltpu.VMEM((2, modes // 2 * CHUNKS, LANES), F32),
            pltpu.VMEM((positions, LANES), F32),
            pltpu.VMEM((positions, LANES), F32),
            pltpu.VMEM((positions, LANES), F32),
            pltpu.VMEM((blocks, CHUNKS, out_rows, LANES), BF16),
            dma,
            dma((2, 2)),
            dma((2, 2)),
            dma((w_chunks,)),
            dma((w_chunks,)),
            dma((w_chunks,)),
            dma((2, 2, 3 * GROUPS)),
            dma((2, 2, 3 * GROUPS)),
            dma((2 * pieces,)),
            dma((2 * pieces,)),
            dma((pieces,)),
            dma((pieces,)),
            dma((pieces,)),
            dma((pieces,)),
            dma,
            dma,
            dma((2,)),
            dma((2,)),
            dma,
            dma,
        ],
        compiler_params=pltpu.CompilerParams(
            collective_id=0, has_side_effects=True, vmem_limit_bytes=64 * 1024 * 1024 - 65536
        ),
    )(x_codes, w_codes, req_mult, req_shift, short_codes, residue_codes, rates, skip_gain.reshape(1, -1))


def solution(mesh):
    placed = (
        P("seq", "tp"),
        P(None, "tp", "seq"),
        P(None, "seq"),
        P(None, "seq"),
        P(None, None, "seq"),
        P(None, "seq"),
        P(None, "seq"),
        P("seq"),
    )
    return jax.shard_map(
        on_device, mesh=mesh, in_specs=placed, out_specs=P(("seq", "tp"), None), check_vma=False
    )
```

```python
import functools
import math

import jax
import jax.numpy as jnp
from jax import lax
from jax.experimental import pallas as pl
from jax.experimental.pallas import tpu as pltpu
from jax.sharding import PartitionSpec as P

MESH = pl.DeviceIdType.MESH
F32 = jnp.float32
BF16 = jnp.bfloat16
LANES = 128
CHUNKS = 8
RING = 4
GROUPS = 5
LATE = 512
WHOLE_FROM = 3
LEAD_BLOCKS = 4


def halves_of(which, array):
    return jnp.where(which == 0, array[..., :LANES], array[..., LANES:])


def small_expm1_neg(z):
    poly = jnp.ones_like(z)
    for order in range(8, 1, -1):
        poly = 1.0 - (z * (1.0 / order)) * poly
    return z * poly


def hyena_kernel(
    x_hbm, w_hbm, mult_hbm, shift_hbm, short_hbm, residue_hbm, rates_hbm, skip_hbm,
    out_ref,
    mult_ref, shift_ref, short_ref, residue_ref, rates_ref, skip_ref, small_sem,
    raw_x, own_x, all_x, raw_w, both_w, sums, near_codes, near_steps, far_codes, far_steps, coded, tails, sib_tails, ends, sib_ends,
    starts, queries, drives, gated, staged,
    x_sem, first_send, first_recv, raw_sem, w_send, w_recv, ring_send, ring_recv, late_send, late_recv,
    far_send, far_recv, step_send, step_recv, tail_send, tail_recv, end_send, end_recv, out_send, out_recv,
):
    seq = lax.axis_index("seq")
    tp = lax.axis_index("tp")
    y = lax.rem(seq, 4)
    layer = lax.rem(seq // 4, 2)
    x = seq // 8
    core = lax.rem(tp, 2)
    high = tp // 2
    rows, feats = own_x.shape
    half_rows = rows // 2
    early = feats - LATE
    modes = residue_ref.shape[0]
    step_count = coded.shape[1] // CHUNKS

    def device(x_at, y_at, layer_at, high_at, core_at):
        return ((x_at * 2 + layer_at) * 4 + y_at, high_at * 2 + core_at)

    def wrap(value):
        return lax.rem(value + 2 * RING, RING)

    barrier = pltpu.get_barrier_semaphore()
    column = layer * 2 + high * 4 + core

    def greet(target):
        pl.semaphore_signal(barrier, inc=1, device_id=target, device_id_type=MESH)

    for offset in range(1, 8):
        other = lax.rem(column + offset, 8)
        greet(device(x, y, lax.rem(other // 2, 2), other // 4, lax.rem(other, 2)))
    for step in (1, RING - 1):
        greet(device(wrap(x + step), y, layer, high, core))
        greet(device(x, wrap(y + step), layer, high, core))

    raw_copy = pltpu.make_async_copy(x_hbm, raw_x, x_sem)
    raw_copy.start()
    w_chunks = raw_w.shape[0]
    w_rows = raw_w.shape[2]
    for chunk in range(w_chunks):
        pltpu.make_async_copy(
            w_hbm.at[:, pl.ds(chunk * w_rows, w_rows), :], raw_w.at[chunk], raw_sem.at[chunk]
        ).start()

    small_copies = [
        pltpu.make_async_copy(source, target, small_sem.at[number])
        for number, (source, target) in enumerate(
            [
                (mult_hbm, mult_ref), (shift_hbm, shift_ref), (short_hbm, short_ref),
                (residue_hbm, residue_ref), (rates_hbm, rates_ref), (skip_hbm, skip_ref),
            ]
        )
    ]
    for copy in small_copies:
        copy.start()
    raw_copy.wait()
    own_x[...] = raw_x[...].astype(F32).astype(BF16)

    def convert_chunk(chunk):
        pltpu.make_async_copy(
            w_hbm.at[:, pl.ds(chunk * w_rows, w_rows), :], raw_w.at[chunk], raw_sem.at[chunk]
        ).wait()
        for which in range(3):
            for half in range(2):
                place = pl.multiple_of((half ^ high) * (3 * LANES) + which * LANES, LANES)
                both_w[core, pl.ds(pl.multiple_of(chunk * w_rows, w_rows), w_rows), pl.ds(place, LANES)] = (
                    raw_w[chunk, which, :, half * LANES : (half + 1) * LANES].astype(F32).astype(BF16)
                )

    pl.semaphore_wait(barrier, 11)

    home = x * 4 + y

    def by_width(group, action):
        whole = jnp.logical_or(core == layer, jnp.asarray(group >= WHOLE_FROM))

        @pl.when(whole)
        def _():
            action(feats)

        @pl.when(jnp.logical_not(whole))
        def _():
            action(early)

    def first_copy(part, across):
        at = pl.ds(part * half_rows, half_rows)
        lanes = pl.ds(0, early if across else feats)
        return pltpu.make_async_remote_copy(
            src_ref=own_x.at[at, lanes], dst_ref=all_x.at[home, core, at, lanes],
            send_sem=first_send.at[int(across), part], recv_sem=first_recv.at[core, part],
            device_id=device(x, y, 1 - layer if across else layer, high, layer), device_id_type=MESH,
        )

    for part in range(2):
        @pl.when(core == layer)
        def _():
            at = pl.ds(part * half_rows, half_rows)
            pltpu.make_async_copy(
                own_x.at[at, :], all_x.at[home, core, at, :], first_recv.at[core, part]
            ).start()

        @pl.when(core != layer)
        def _():
            first_copy(part, False).start()

        first_copy(part, True).start()

    sibling = device(x, y, layer, high, 1 - core)

    def w_copy(chunk):
        piece = both_w.at[core, pl.ds(pl.multiple_of(chunk * w_rows, w_rows), w_rows), :]
        return pltpu.make_async_remote_copy(
            src_ref=piece, dst_ref=piece, send_sem=w_send.at[chunk], recv_sem=w_recv.at[chunk],
            device_id=sibling, device_id_type=MESH,
        )

    def w_arrival(chunk):
        piece = both_w.at[1 - core, pl.ds(pl.multiple_of(chunk * w_rows, w_rows), w_rows), :]
        return pltpu.make_async_remote_copy(
            src_ref=piece, dst_ref=piece, send_sem=w_send.at[chunk], recv_sem=w_recv.at[chunk],
            device_id=sibling, device_id_type=MESH,
        )

    def piece_of(axis, group, along):
        shifted = jnp.maximum(group - 1, 0)
        first = jnp.where(group == 0, 1, 0)
        if axis == 0:
            return wrap(x + along) * 4 + wrap(y + shifted), 1 - first
        return wrap(x + shifted) * 4 + wrap(y + along), first

    def part_rows(part):
        return pl.ds(pl.multiple_of(part * half_rows, half_rows), half_rows)

    def ring_copy(axis, way, group, turn, along, feat, width):
        slot, part = piece_of(axis, group, along)
        unit = all_x.at[slot, feat, part_rows(part), pl.ds(0, width)]
        step = 1 if way == 0 else -1
        target = (
            device(wrap(x + step), y, layer, high, core)
            if axis == 0
            else device(x, wrap(y + step), layer, high, core)
        )
        return pltpu.make_async_remote_copy(
            src_ref=unit, dst_ref=unit,
            send_sem=ring_send.at[axis, way, group * 3 + turn],
            recv_sem=ring_recv.at[axis, way, group * 3 + turn],
            device_id=target, device_id_type=MESH,
        )

    def own_feat(turn):
        return core if turn == 0 else 1 - core

    def send_own(group, width, axes=(0, 1), turns=(0, 1)):
        for turn in turns:
            for axis in axes:
                for way in range(2):
                    ring_copy(axis, way, group, turn, 0, own_feat(turn), width).start()

    def send_on(group, width):
        for axis in range(2):
            for way in range(2):
                ring_copy(axis, way, group, 2, -1 if way == 0 else 1, way, width).start()

    def wait_own(group, width):
        for turn in range(2):
            for axis in range(2):
                for way in range(2):
                    ring_copy(axis, way, group, turn, -1 if way == 0 else 1, own_feat(turn), width).wait_recv()

    def wait_on(group, width):
        for axis in range(2):
            for way in range(2):
                ring_copy(axis, way, group, 2, 2, way, width).wait_recv()

    def late_copies(pieces):
        for slot, part in pieces:
            for feat in range(2):
                place = all_x.at[slot, feat, part_rows(part), pl.ds(early, LATE)]
                number = slot * 4 + part * 2 + feat
                yield pltpu.make_async_remote_copy(
                    src_ref=place, dst_ref=place,
                    send_sem=late_send.at[number], recv_sem=late_recv.at[number],
                    device_id=device(x, y, 1 - layer, high, core), device_id_type=MESH,
                )

    def send_late(pieces):
        @pl.when(core == layer)
        def _():
            for copy in late_copies(pieces):
                copy.start()

    def wait_late(pieces):
        @pl.when(core != layer)
        def _():
            for copy in late_copies(pieces):
                copy.wait_recv()

    far_home = device(x, y, layer, 1 - high, core)

    def far_copies(row):
        piece = row // half_rows
        return (
            pltpu.make_async_remote_copy(
                src_ref=near_codes.at[piece], dst_ref=far_codes.at[piece],
                send_sem=far_send.at[piece], recv_sem=far_recv.at[piece],
                device_id=far_home, device_id_type=MESH,
            ),
            pltpu.make_async_remote_copy(
                src_ref=near_steps.at[piece], dst_ref=far_steps.at[piece],
                send_sem=step_send.at[piece], recv_sem=step_recv.at[piece],
                device_id=far_home, device_id_type=MESH,
            ),
        )

    def multiply(pieces):
        total = None
        for feat in range(2):
            left = jnp.concatenate(
                [
                    all_x[slot, feat, part_rows(part), :]
                    for slot, part in pieces
                ],
                axis=0,
            )
            term = jnp.dot(left, both_w[feat], preferred_element_type=F32)
            total = term if total is None else total + term
        for index, (slot, part) in enumerate(pieces):
            row = pl.multiple_of(slot * rows + part * half_rows, half_rows)
            part_sums = total[index * half_rows : (index + 1) * half_rows]
            sums[pl.ds(row, half_rows), :] = part_sums[:, : 3 * LANES]
            away = part_sums[:, 3 * LANES :]
            peak = jnp.maximum(jnp.max(jnp.abs(away), axis=0, keepdims=True), 1.0)
            near_steps[row // half_rows] = peak * (1.0 / 32767.0)
            scaled = jnp.round(away * (32767.0 / peak))
            near_codes[row // half_rows] = scaled.astype(jnp.int32).astype(jnp.int16)
        for slot, part in pieces:
            for copy in far_copies(slot * rows + part * half_rows):
                copy.start()

    def finish(pieces):
        for slot, part in pieces:
            piece = slot * 2 + part
            for copy in far_copies(piece * half_rows):
                copy.wait_recv()
            at = pl.ds(pl.multiple_of(piece * half_rows, half_rows), half_rows)
            for which in range(3):
                lanes = slice(which * LANES, (which + 1) * LANES)
                away = far_codes[piece, :, lanes].astype(jnp.int32).astype(F32) * far_steps[piece, :, lanes]
                total = (sums[at, lanes] + away) * requant[which : which + 1, :]
                coded[which, at, :] = jnp.clip(total, -127.0, 127.0).astype(BF16).astype(F32)

    def near_pieces(group):
        return [piece_of(axis, group, along) for axis in range(2) for along in (-1, 1)]

    def next_pieces(group):
        return [piece_of(axis, group, 2) for axis in range(2)]

    def second_pieces(group):
        start = group == 0
        return [
            (jnp.where(start, home, slot), jnp.where(start, axis, part))
            for axis, (slot, part) in enumerate(next_pieces(jnp.maximum(group - 1, 0)))
        ]

    def begin_ring(width):
        for part in range(2):
            for turn in range(2):
                feat = own_feat(turn)
                landed = all_x.at[home, feat, pl.ds(part * half_rows, half_rows), pl.ds(0, width)]
                pltpu.make_async_copy(landed, landed, first_recv.at[feat, part]).wait()
                send_own(0, width, (part,), (turn,))
        send_own(1, width)

    @pl.when(core == layer)
    def _():
        for turn in range(2):
            feat = own_feat(turn)
            for part in range(2):
                landed = all_x.at[home, feat, pl.ds(part * half_rows, half_rows), :]
                pltpu.make_async_copy(landed, landed, first_recv.at[feat, part]).wait()
                send_own(0, feats, (part,), (turn,))
        send_own(1, feats)

    for copy in small_copies:
        copy.wait()
    requant = halves_of(high, mult_ref[...].astype(F32) * jnp.exp2(-shift_ref[...].astype(F32)))
    taps = halves_of(high, short_ref[...].astype(F32) * (1.0 / 8192.0))
    rates = halves_of(high, rates_ref[...])
    coeffs = (
        halves_of(high, residue_ref[...].astype(F32))
        * (1.0 / (127.0 * math.sqrt(modes)))
        * jnp.sqrt(small_expm1_neg(2.0 * rates))
    )
    skip = halves_of(high, skip_ref[...])
    decays = jnp.exp(-rates)
    fix_decays = jnp.exp(-rates * float(step_count - 2))
    chunk_decays = jnp.exp(-rates * float(step_count))

    @pl.loop(0, w_chunks)
    def _(chunk):
        convert_chunk(chunk)
        w_copy(chunk).start()

    @pl.when(core != layer)
    def _():
        begin_ring(early)

    @pl.loop(0, GROUPS)
    def _(group):
        def first_half(width):
            wait_own(group, width)
            send_on(group, width)

        by_width(group, first_half)
        near = near_pieces(group)

        @pl.when(group < WHOLE_FROM)
        def _():
            send_late(near)

        @pl.when(group == 0)
        def _():
            @pl.loop(0, w_chunks)
            def _(chunk):
                w_arrival(chunk).wait_recv()

        @pl.when(group < WHOLE_FROM)
        def _():
            wait_late(near)

        multiply(near)

        @pl.when(group > 0)
        def _():
            finish(near_pieces(group - 1))

        @pl.when(group > 0)
        def _():
            by_width(group - 1, lambda width: wait_on(group - 1, width))

        second = second_pieces(group)

        @pl.when(group <= WHOLE_FROM)
        def _():
            send_late(second)
            wait_late(second)

        @pl.when(group + 2 < GROUPS)
        def _():
            by_width(group + 2, lambda width: send_own(group + 2, width))

        multiply(second)

        @pl.when(group > 0)
        def _():
            finish(second_pieces(group - 1))

    finish(near_pieces(GROUPS - 1))

    for part in range(2):
        first_copy(part, True).wait_send()

        @pl.when(core != layer)
        def _():
            first_copy(part, False).wait_send()

    @pl.loop(0, w_chunks)
    def _(chunk):
        w_copy(chunk).wait_send()

    def sent_turn(group, turn, width):
        for axis in range(2):
            for way in range(2):
                ring_copy(axis, way, group, turn, 0, 0, width).wait_send()

    @pl.loop(0, GROUPS)
    def _(group):
        def sent_own(width):
            for turn in range(2):
                sent_turn(group, turn, width)

        by_width(group, sent_own)

    @pl.loop(0, GROUPS - 1)
    def _(group):
        by_width(group, lambda width: sent_turn(group, 2, width))

    @pl.when(core == layer)
    def _():
        for copy in late_copies([(home, 0), (home, 1)]):
            copy.wait_send()

        @pl.loop(0, WHOLE_FROM)
        def _(group):
            for copy in late_copies(near_pieces(group) + next_pieces(group)):
                copy.wait_send()

    by_width(GROUPS - 1, lambda width: wait_on(GROUPS - 1, width))
    last = next_pieces(GROUPS - 1)
    multiply(last)
    finish(second_pieces(GROUPS - 1))
    by_width(GROUPS - 1, lambda width: sent_turn(GROUPS - 1, 2, width))

    @pl.loop(0, near_codes.shape[0])
    def _(piece):
        for copy in far_copies(piece * half_rows):
            copy.wait_send()

    finish(last)

    for back in range(2):
        for which in range(3):
            tails[back, which] = coded[which, pl.ds(step_count - 1 - back, CHUNKS, stride=step_count), :]
    tail_copy = pltpu.make_async_remote_copy(
        src_ref=tails, dst_ref=sib_tails, send_sem=tail_send, recv_sem=tail_recv,
        device_id=sibling, device_id_type=MESH,
    )
    tail_copy.start()

    def spread(row):
        return jnp.broadcast_to(row, (CHUNKS, LANES))

    tap_rows = [[spread(taps[lag, which : which + 1, :]) for which in range(3)] for lag in range(3)]
    decay_rows = [spread(decays[mode : mode + 1, :]) for mode in range(modes)]
    index = lax.broadcasted_iota(jnp.int32, (CHUNKS, LANES), 0)
    odd = lax.rem(index, 2) == 1

    def before_chunk(back, which):
        own = pltpu.roll(tails[back, which], 1, 0)
        other = sib_tails[back, which]
        up = pltpu.roll(other, 1, 0)
        down = pltpu.roll(other, CHUNKS - 1, 0)
        outside = jnp.where(core == 0, jnp.where(index == 0, 0.0, up), down)
        return jnp.where(odd, own, outside)

    half_modes = modes // 2

    def load_step(step):
        return tuple(coded[which, pl.ds(step, CHUNKS, stride=step_count), :] for which in range(3))

    def featurize(step, now, newer, older):
        feat = [
            tap_rows[0][which] * now[which]
            + tap_rows[1][which] * newer[which]
            + tap_rows[2][which] * older[which]
            for which in range(3)
        ]
        drive = feat[1] * feat[2]
        at = pl.ds(pl.multiple_of(step * CHUNKS, CHUNKS), CHUNKS)
        queries[at, :] = feat[0]
        drives[at, :] = drive
        return drive

    def advance(states, drive, half):
        return tuple(
            decay_rows[half * half_modes + mode] * states[mode] + drive for mode in range(half_modes)
        )

    def first_pass(step, carry):
        older, newer, states = carry
        now = load_step(step)
        drive = featurize(step, now, newer, older)
        return newer, now, advance(states, drive, 0)

    def load_drive(step):
        return drives[pl.ds(pl.multiple_of(step * CHUNKS, CHUNKS), CHUNKS), :]

    def send_ends(half, states):
        for mode in range(half_modes):
            ends[half, mode * CHUNKS : (mode + 1) * CHUNKS, :] = states[mode]
        end_copy(half).start()

    def end_copy(half):
        return pltpu.make_async_remote_copy(
            src_ref=ends.at[half], dst_ref=sib_ends.at[half],
            send_sem=end_send.at[half], recv_sem=end_recv.at[half],
            device_id=sibling, device_id_type=MESH,
        )

    def start_states(half):
        end_copy(half).wait_recv()
        state = jnp.zeros((half_modes, LANES), F32)
        ratio = chunk_decays[half * half_modes : (half + 1) * half_modes, :]
        for run in range(CHUNKS // 2):
            for owner in range(2):
                for chunk in (2 * run, 2 * run + 1):
                    rows_at = pl.ds(chunk, half_modes, stride=CHUNKS)
                    starts[owner, rows_at, :] = state
                    ended = jnp.where(core == owner, ends[half, rows_at, :], sib_ends[half, rows_at, :])
                    state = ratio * state + ended
        return tuple(starts[core, mode * CHUNKS : (mode + 1) * CHUNKS, :] for mode in range(half_modes))

    zeros = tuple(jnp.zeros((CHUNKS, LANES), F32) for _ in range(half_modes))
    step_0, step_1 = load_step(0), load_step(1)
    _, _, states = lax.fori_loop(2, step_count, first_pass, (step_0, step_1, zeros), unroll=2)
    tail_copy.wait_recv()
    back_1 = tuple(before_chunk(0, which) for which in range(3))
    back_2 = tuple(before_chunk(1, which) for which in range(3))
    drive_0 = featurize(0, step_0, back_1, back_2)
    drive_1 = featurize(1, step_1, step_0, back_1)
    states = tuple(
        states[mode] + spread(fix_decays[mode : mode + 1, :]) * (decay_rows[mode] * drive_0 + drive_1)
        for mode in range(half_modes)
    )
    send_ends(0, states)
    states = lax.fori_loop(
        0, step_count, lambda step, held: advance(held, load_drive(step), 1), zeros, unroll=4
    )
    send_ends(1, states)
    coeff_rows = [spread(coeffs[mode : mode + 1, :]) for mode in range(modes)]
    skip_row = spread(skip)

    def weigh(states, half):
        parts = [coeff_rows[half * half_modes + mode] * states[mode] for mode in range(half_modes)]
        while len(parts) > 1:
            parts = [parts[i] + parts[i + 1] for i in range(0, len(parts), 2)]
        return parts[0]

    def middle_pass(step, states):
        at = pl.ds(pl.multiple_of(step * CHUNKS, CHUNKS), CHUNKS)
        drive = drives[at, :]
        states = advance(states, drive, 0)
        gated[at, :] = weigh(states, 0) + skip_row * drive
        return states

    lead = LEAD_BLOCKS * (step_count // 8)
    held_0 = lax.fori_loop(0, lead, middle_pass, start_states(0), unroll=4)

    out_rows = out_ref.shape[0]
    blocks = step_count // out_rows
    channel = pl.multiple_of((seq * 2 + high) * LANES, LANES)

    def second_pass(step, states):
        at = pl.ds(pl.multiple_of(step * CHUNKS, CHUNKS), CHUNKS)
        states = advance(states, drives[at, :], 1)
        gated[at, :] = queries[at, :] * (gated[at, :] + weigh(states, 1))
        return states

    place = out_ref.at[:, pl.ds(channel, LANES)]
    first_seat = core * 4

    def send_outs(block):
        row = first_seat + block // 4
        tp_at = lax.rem(block, 4)
        for chunk in range(CHUNKS):
            seq_at = row + (chunk // 2) * 8 + (chunk % 2) * 2
            is_me = jnp.logical_and(seq_at == seq, tp_at == tp)

            @pl.when(is_me)
            def _():
                pltpu.make_async_copy(staged.at[block, chunk], place, out_recv).start()

            @pl.when(jnp.logical_not(is_me))
            def _():
                pltpu.make_async_remote_copy(
                    src_ref=staged.at[block, chunk], dst_ref=place, send_sem=out_send, recv_sem=out_recv,
                    device_id=(seq_at, tp_at), device_id_type=MESH,
                ).start()

    def whole_pass(step, both):
        at = pl.ds(pl.multiple_of(step * CHUNKS, CHUNKS), CHUNKS)
        drive = drives[at, :]
        states_0, states_1 = advance(both[0], drive, 0), advance(both[1], drive, 1)
        total = (weigh(states_0, 0) + skip_row * drive) + weigh(states_1, 1)
        gated[at, :] = queries[at, :] * total
        return states_0, states_1

    def out_block(block, states, step_pass):
        states = lax.fori_loop(
            0, out_rows, lambda step, held: step_pass(block * out_rows + step, held), states, unroll=4
        )
        for chunk in range(CHUNKS):
            taken = gated[pl.ds(block * (out_rows * CHUNKS) + chunk, out_rows, stride=CHUNKS), :]
            staged[block, chunk] = taken.astype(BF16)
        send_outs(block)
        return states

    held_1 = lax.fori_loop(
        0, LEAD_BLOCKS, lambda block, held: out_block(block, held, second_pass), start_states(1)
    )
    lax.fori_loop(
        LEAD_BLOCKS, blocks, lambda block, held: out_block(block, held, whole_pass), (held_0, held_1)
    )

    tail_copy.wait_send()
    for half in range(2):
        end_copy(half).wait_send()
    pltpu.make_async_copy(out_ref, out_ref, out_recv).wait()
    sent = staged.at[pl.ds(1, blocks - 1)]
    pltpu.make_async_copy(sent, sent, out_send).wait()
    most = staged.at[0, pl.ds(1, CHUNKS - 1)]
    pltpu.make_async_copy(most, most, out_send).wait()

    @pl.when(core != layer)
    def _():
        pltpu.make_async_copy(staged.at[0, 0], staged.at[0, 0], out_send).wait()


def on_device(x_codes, w_codes, req_mult, req_shift, short_codes, residue_codes, rates, skip_gain):
    rows, feats = x_codes.shape
    seq_devs = lax.axis_size("seq")
    tp_devs = lax.axis_size("tp")
    cols = w_codes.shape[2]
    positions = rows * seq_devs // 2
    modes = residue_codes.shape[0]
    out_rows = rows // tp_devs
    steps = positions // CHUNKS
    blocks = steps // out_rows
    pieces = 2 * positions // rows
    w_rows = 256
    w_chunks = feats // w_rows
    small = (req_mult, req_shift, short_codes, residue_codes, rates, skip_gain.reshape(1, -1))
    dma = pltpu.SemaphoreType.DMA
    return pl.pallas_call(
        hyena_kernel,
        out_shape=pltpu.VMEM((out_rows, cols * seq_devs), BF16),
        in_specs=[pl.BlockSpec(memory_space=pl.ANY)] * 8,
        out_specs=pl.BlockSpec(memory_space=pltpu.VMEM),
        scratch_shapes=[
            *(pltpu.VMEM(array.shape, array.dtype) for array in small),
            dma((len(small),)),
            pltpu.VMEM((rows, feats), jnp.int32),
            pltpu.VMEM((rows, feats), BF16),
            pltpu.VMEM((seq_devs // 2, 2, rows, feats), BF16),
            pltpu.VMEM((w_chunks, 3, w_rows, cols), jnp.int32),
            pltpu.VMEM((2, feats, 3 * cols), BF16),
            pltpu.VMEM((positions, 3 * LANES), F32),
            pltpu.VMEM((pieces, rows // 2, 3 * LANES), jnp.int16),
            pltpu.VMEM((pieces, 1, 3 * LANES), F32),
            pltpu.VMEM((pieces, rows // 2, 3 * LANES), jnp.int16),
            pltpu.VMEM((pieces, 1, 3 * LANES), F32),
            pltpu.VMEM((3, positions, LANES), F32),
            pltpu.VMEM((2, 3, CHUNKS, LANES), F32),
            pltpu.VMEM((2, 3, CHUNKS, LANES), F32),
            pltpu.VMEM((2, modes // 2 * CHUNKS, LANES), F32),
            pltpu.VMEM((2, modes // 2 * CHUNKS, LANES), F32),
            pltpu.VMEM((2, modes // 2 * CHUNKS, LANES), F32),
            pltpu.VMEM((positions, LANES), F32),
            pltpu.VMEM((positions, LANES), F32),
            pltpu.VMEM((positions, LANES), F32),
            pltpu.VMEM((blocks, CHUNKS, out_rows, LANES), BF16),
            dma,
            dma((2, 2)),
            dma((2, 2)),
            dma((w_chunks,)),
            dma((w_chunks,)),
            dma((w_chunks,)),
            dma((2, 2, 3 * GROUPS)),
            dma((2, 2, 3 * GROUPS)),
            dma((2 * pieces,)),
            dma((2 * pieces,)),
            dma((pieces,)),
            dma((pieces,)),
            dma((pieces,)),
            dma((pieces,)),
            dma,
            dma,
            dma((2,)),
            dma((2,)),
            dma,
            dma,
        ],
        compiler_params=pltpu.CompilerParams(
            collective_id=0, has_side_effects=True, vmem_limit_bytes=56 * 1024 * 1024
        ),
    )(x_codes, w_codes, *small)


def solution(mesh):
    placed = (
        P("seq", "tp"),
        P(None, "tp", "seq"),
        P(None, "seq"),
        P(None, "seq"),
        P(None, None, "seq"),
        P(None, "seq"),
        P(None, "seq"),
        P("seq"),
    )
    return jax.shard_map(
        on_device, mesh=mesh, in_specs=placed, out_specs=P(("seq", "tp"), None), check_vma=False
    )
```

```python
import functools
import math

import jax
import jax.numpy as jnp
from jax import lax
from jax.experimental import pallas as pl
from jax.experimental.pallas import tpu as pltpu
from jax.sharding import PartitionSpec as P

MESH = pl.DeviceIdType.MESH
F32 = jnp.float32
BF16 = jnp.bfloat16
LANES = 128
CHUNKS = 8
RING = 4
GROUPS = 5
LATE = 512
WHOLE_FROM = 3
LEAD_BLOCKS = 4


def halves_of(which, array):
    return jnp.where(which == 0, array[..., :LANES], array[..., LANES:])


def small_expm1_neg(z):
    poly = jnp.ones_like(z)
    for order in range(8, 1, -1):
        poly = 1.0 - (z * (1.0 / order)) * poly
    return z * poly


def hyena_kernel(
    x_hbm, w_hbm, mult_hbm, shift_hbm, short_hbm, residue_hbm, rates_hbm, skip_hbm,
    out_ref,
    mult_ref, shift_ref, short_ref, residue_ref, rates_ref, skip_ref, small_sem,
    raw_x, own_x, all_x, raw_w, both_w, sums, near_codes, near_steps, far_codes, far_steps, coded, tails, sib_tails, ends, sib_ends,
    starts, queries, drives, gated, staged,
    x_sem, first_send, first_recv, raw_sem, w_send, w_recv, ring_send, ring_recv, late_send, late_recv,
    far_send, far_recv, step_send, step_recv, tail_send, tail_recv, end_send, end_recv, out_send, out_recv,
):
    seq = lax.axis_index("seq")
    tp = lax.axis_index("tp")
    y = lax.rem(seq, 4)
    layer = lax.rem(seq // 4, 2)
    x = seq // 8
    core = lax.rem(tp, 2)
    high = tp // 2
    rows, feats = own_x.shape
    half_rows = rows // 2
    early = feats - LATE
    modes = residue_ref.shape[0]
    step_count = coded.shape[1] // CHUNKS

    def device(x_at, y_at, layer_at, high_at, core_at):
        return ((x_at * 2 + layer_at) * 4 + y_at, high_at * 2 + core_at)

    def wrap(value):
        return lax.rem(value + 2 * RING, RING)

    barrier = pltpu.get_barrier_semaphore()
    column = layer * 2 + high * 4 + core

    def greet(target):
        pl.semaphore_signal(barrier, inc=1, device_id=target, device_id_type=MESH)

    for offset in range(1, 8):
        other = lax.rem(column + offset, 8)
        greet(device(x, y, lax.rem(other // 2, 2), other // 4, lax.rem(other, 2)))
    for step in (1, RING - 1):
        greet(device(wrap(x + step), y, layer, high, core))
        greet(device(x, wrap(y + step), layer, high, core))

    raw_copy = pltpu.make_async_copy(x_hbm, raw_x, x_sem)
    raw_copy.start()
    w_chunks = raw_w.shape[0]
    w_rows = raw_w.shape[2]
    for chunk in range(w_chunks):
        pltpu.make_async_copy(
            w_hbm.at[:, pl.ds(chunk * w_rows, w_rows), :], raw_w.at[chunk], raw_sem.at[chunk]
        ).start()

    small_copies = [
        pltpu.make_async_copy(source, target, small_sem.at[number])
        for number, (source, target) in enumerate(
            [
                (mult_hbm, mult_ref), (shift_hbm, shift_ref), (short_hbm, short_ref),
                (residue_hbm, residue_ref), (rates_hbm, rates_ref), (skip_hbm, skip_ref),
            ]
        )
    ]
    for copy in small_copies:
        copy.start()
    raw_copy.wait()
    own_x[...] = raw_x[...].astype(F32).astype(BF16)

    def convert_chunk(chunk):
        pltpu.make_async_copy(
            w_hbm.at[:, pl.ds(chunk * w_rows, w_rows), :], raw_w.at[chunk], raw_sem.at[chunk]
        ).wait()
        for which in range(3):
            for half in range(2):
                place = pl.multiple_of((half ^ high) * (3 * LANES) + which * LANES, LANES)
                both_w[core, pl.ds(pl.multiple_of(chunk * w_rows, w_rows), w_rows), pl.ds(place, LANES)] = (
                    raw_w[chunk, which, :, half * LANES : (half + 1) * LANES].astype(F32).astype(BF16)
                )

    pl.semaphore_wait(barrier, 11)

    home = x * 4 + y

    def by_width(group, action):
        whole = jnp.logical_or(core == layer, jnp.asarray(group >= WHOLE_FROM))

        @pl.when(whole)
        def _():
            action(feats)

        @pl.when(jnp.logical_not(whole))
        def _():
            action(early)

    def first_copy(part, across):
        at = pl.ds(part * half_rows, half_rows)
        lanes = pl.ds(0, early if across else feats)
        return pltpu.make_async_remote_copy(
            src_ref=own_x.at[at, lanes], dst_ref=all_x.at[home, core, at, lanes],
            send_sem=first_send.at[int(across), part], recv_sem=first_recv.at[core, part],
            device_id=device(x, y, 1 - layer if across else layer, high, layer), device_id_type=MESH,
        )

    for part in range(2):
        @pl.when(core == layer)
        def _():
            at = pl.ds(part * half_rows, half_rows)
            pltpu.make_async_copy(
                own_x.at[at, :], all_x.at[home, core, at, :], first_recv.at[core, part]
            ).start()

        @pl.when(core != layer)
        def _():
            first_copy(part, False).start()

        first_copy(part, True).start()

    sibling = device(x, y, layer, high, 1 - core)

    def w_copy(chunk):
        piece = both_w.at[core, pl.ds(pl.multiple_of(chunk * w_rows, w_rows), w_rows), :]
        return pltpu.make_async_remote_copy(
            src_ref=piece, dst_ref=piece, send_sem=w_send.at[chunk], recv_sem=w_recv.at[chunk],
            device_id=sibling, device_id_type=MESH,
        )

    def w_arrival(chunk):
        piece = both_w.at[1 - core, pl.ds(pl.multiple_of(chunk * w_rows, w_rows), w_rows), :]
        return pltpu.make_async_remote_copy(
            src_ref=piece, dst_ref=piece, send_sem=w_send.at[chunk], recv_sem=w_recv.at[chunk],
            device_id=sibling, device_id_type=MESH,
        )

    def piece_of(axis, group, along):
        shifted = jnp.maximum(group - 1, 0)
        first = jnp.where(group == 0, 1, 0)
        if axis == 0:
            return wrap(x + along) * 4 + wrap(y + shifted), 1 - first
        return wrap(x + shifted) * 4 + wrap(y + along), first

    def part_rows(part):
        return pl.ds(pl.multiple_of(part * half_rows, half_rows), half_rows)

    def ring_copy(axis, way, group, turn, along, feat, width):
        slot, part = piece_of(axis, group, along)
        unit = all_x.at[slot, feat, part_rows(part), pl.ds(0, width)]
        step = 1 if way == 0 else -1
        target = (
            device(wrap(x + step), y, layer, high, core)
            if axis == 0
            else device(x, wrap(y + step), layer, high, core)
        )
        return pltpu.make_async_remote_copy(
            src_ref=unit, dst_ref=unit,
            send_sem=ring_send.at[axis, way, group * 3 + turn],
            recv_sem=ring_recv.at[axis, way, group * 3 + turn],
            device_id=target, device_id_type=MESH,
        )

    def own_feat(turn):
        return core if turn == 0 else 1 - core

    def send_own(group, width, axes=(0, 1), turns=(0, 1)):
        for turn in turns:
            for axis in axes:
                for way in range(2):
                    ring_copy(axis, way, group, turn, 0, own_feat(turn), width).start()

    def send_on(group, width):
        for axis in range(2):
            for way in range(2):
                ring_copy(axis, way, group, 2, -1 if way == 0 else 1, way, width).start()

    def wait_own(group, width):
        for turn in range(2):
            for axis in range(2):
                for way in range(2):
                    ring_copy(axis, way, group, turn, -1 if way == 0 else 1, own_feat(turn), width).wait_recv()

    def wait_on(group, width):
        for axis in range(2):
            for way in range(2):
                ring_copy(axis, way, group, 2, 2, way, width).wait_recv()

    def late_copies(pieces):
        for slot, part in pieces:
            for feat in range(2):
                place = all_x.at[slot, feat, part_rows(part), pl.ds(early, LATE)]
                number = slot * 4 + part * 2 + feat
                yield pltpu.make_async_remote_copy(
                    src_ref=place, dst_ref=place,
                    send_sem=late_send.at[number], recv_sem=late_recv.at[number],
                    device_id=device(x, y, 1 - layer, high, core), device_id_type=MESH,
                )

    def send_late(pieces):
        @pl.when(core == layer)
        def _():
            for copy in late_copies(pieces):
                copy.start()

    def wait_late(pieces):
        @pl.when(core != layer)
        def _():
            for copy in late_copies(pieces):
                copy.wait_recv()

    far_home = device(x, y, layer, 1 - high, core)

    def far_copies(row):
        piece = row // half_rows
        return (
            pltpu.make_async_remote_copy(
                src_ref=near_codes.at[piece], dst_ref=far_codes.at[piece],
                send_sem=far_send.at[piece], recv_sem=far_recv.at[piece],
                device_id=far_home, device_id_type=MESH,
            ),
            pltpu.make_async_remote_copy(
                src_ref=near_steps.at[piece], dst_ref=far_steps.at[piece],
                send_sem=step_send.at[piece], recv_sem=step_recv.at[piece],
                device_id=far_home, device_id_type=MESH,
            ),
        )

    def product(pieces, first, stop):
        total = None
        for feat in range(2):
            left = jnp.concatenate(
                [all_x[slot, feat, part_rows(part), :] for slot, part in pieces], axis=0
            )
            term = jnp.dot(left, both_w[feat, :, first:stop], preferred_element_type=F32)
            total = term if total is None else total + term
        return [total[index * half_rows : (index + 1) * half_rows] for index in range(len(pieces))]

    def put_sums(pieces, parts, first):
        for (slot, part), values in zip(pieces, parts):
            row = pl.multiple_of(slot * rows + part * half_rows, half_rows)
            sums[pl.ds(row, half_rows), first : first + values.shape[1]] = values

    def put_codes(pieces, parts):
        for (slot, part), away in zip(pieces, parts):
            piece = slot * 2 + part
            peak = jnp.maximum(jnp.max(jnp.abs(away), axis=0, keepdims=True), 1.0)
            near_steps[piece] = peak * (1.0 / 32767.0)
            near_codes[piece] = jnp.round(away * (32767.0 / peak)).astype(jnp.int32).astype(jnp.int16)
        for slot, part in pieces:
            for copy in far_copies(slot * rows + part * half_rows):
                copy.start()

    def multiply(pieces):
        parts = product(pieces, 0, 6 * LANES)
        put_sums(pieces, [values[:, : 3 * LANES] for values in parts], 0)
        put_codes(pieces, [values[:, 3 * LANES :] for values in parts])

    def multiply_last(pieces):
        parts = product(pieces, 2 * LANES, 6 * LANES)
        put_codes(pieces, [values[:, LANES:] for values in parts])
        put_sums(pieces, [values[:, :LANES] for values in parts], 2 * LANES)
        put_sums(pieces, product(pieces, 0, 2 * LANES), 0)

    def finish(pieces):
        for slot, part in pieces:
            piece = slot * 2 + part
            for copy in far_copies(piece * half_rows):
                copy.wait_recv()
            at = pl.ds(pl.multiple_of(piece * half_rows, half_rows), half_rows)
            for which in range(3):
                lanes = slice(which * LANES, (which + 1) * LANES)
                away = far_codes[piece, :, lanes].astype(jnp.int32).astype(F32) * far_steps[piece, :, lanes]
                total = (sums[at, lanes] + away) * requant[which : which + 1, :]
                coded[which, at, :] = jnp.clip(total, -127.0, 127.0).astype(BF16).astype(F32)

    def near_pieces(group):
        return [piece_of(axis, group, along) for axis in range(2) for along in (-1, 1)]

    def next_pieces(group):
        return [piece_of(axis, group, 2) for axis in range(2)]

    def second_pieces(group):
        start = group == 0
        return [
            (jnp.where(start, home, slot), jnp.where(start, axis, part))
            for axis, (slot, part) in enumerate(next_pieces(jnp.maximum(group - 1, 0)))
        ]

    def begin_ring(width):
        for part in range(2):
            for turn in range(2):
                feat = own_feat(turn)
                landed = all_x.at[home, feat, pl.ds(part * half_rows, half_rows), pl.ds(0, width)]
                pltpu.make_async_copy(landed, landed, first_recv.at[feat, part]).wait()
                send_own(0, width, (part,), (turn,))
        send_own(1, width)

    @pl.when(core == layer)
    def _():
        for turn in range(2):
            feat = own_feat(turn)
            for part in range(2):
                landed = all_x.at[home, feat, pl.ds(part * half_rows, half_rows), :]
                pltpu.make_async_copy(landed, landed, first_recv.at[feat, part]).wait()
                send_own(0, feats, (part,), (turn,))
        send_own(1, feats)

    for copy in small_copies:
        copy.wait()
    requant = halves_of(high, mult_ref[...].astype(F32) * jnp.exp2(-shift_ref[...].astype(F32)))
    taps = halves_of(high, short_ref[...].astype(F32) * (1.0 / 8192.0))
    rates = halves_of(high, rates_ref[...])
    coeffs = (
        halves_of(high, residue_ref[...].astype(F32))
        * (1.0 / (127.0 * math.sqrt(modes)))
        * jnp.sqrt(small_expm1_neg(2.0 * rates))
    )
    skip = halves_of(high, skip_ref[...])
    decays = jnp.exp(-rates)
    fix_decays = jnp.exp(-rates * float(step_count - 2))
    chunk_decays = jnp.exp(-rates * float(step_count))

    @pl.loop(0, w_chunks)
    def _(chunk):
        convert_chunk(chunk)
        w_copy(chunk).start()

    @pl.when(core != layer)
    def _():
        begin_ring(early)

    @pl.loop(0, GROUPS)
    def _(group):
        def first_half(width):
            wait_own(group, width)
            send_on(group, width)

        by_width(group, first_half)
        near = near_pieces(group)

        @pl.when(group < WHOLE_FROM)
        def _():
            send_late(near)

        @pl.when(group == 0)
        def _():
            @pl.loop(0, w_chunks)
            def _(chunk):
                w_arrival(chunk).wait_recv()

        @pl.when(group < WHOLE_FROM)
        def _():
            wait_late(near)

        multiply(near)

        @pl.when(group > 0)
        def _():
            finish(near_pieces(group - 1))

        @pl.when(group > 0)
        def _():
            by_width(group - 1, lambda width: wait_on(group - 1, width))

        second = second_pieces(group)

        @pl.when(group <= WHOLE_FROM)
        def _():
            send_late(second)
            wait_late(second)

        @pl.when(group + 2 < GROUPS)
        def _():
            by_width(group + 2, lambda width: send_own(group + 2, width))

        multiply(second)

        @pl.when(group > 0)
        def _():
            finish(second_pieces(group - 1))

    for part in range(2):
        first_copy(part, True).wait_send()

        @pl.when(core != layer)
        def _():
            first_copy(part, False).wait_send()

    @pl.loop(0, w_chunks)
    def _(chunk):
        w_copy(chunk).wait_send()

    def sent_turn(group, turn, width):
        for axis in range(2):
            for way in range(2):
                ring_copy(axis, way, group, turn, 0, 0, width).wait_send()

    @pl.loop(0, GROUPS)
    def _(group):
        def sent_own(width):
            for turn in range(2):
                sent_turn(group, turn, width)

        by_width(group, sent_own)

    @pl.loop(0, GROUPS - 1)
    def _(group):
        by_width(group, lambda width: sent_turn(group, 2, width))

    @pl.when(core == layer)
    def _():
        for copy in late_copies([(home, 0), (home, 1)]):
            copy.wait_send()

        @pl.loop(0, WHOLE_FROM)
        def _(group):
            for copy in late_copies(near_pieces(group) + next_pieces(group)):
                copy.wait_send()

    by_width(GROUPS - 1, lambda width: wait_on(GROUPS - 1, width))
    last = next_pieces(GROUPS - 1)
    multiply_last(last)
    finish(near_pieces(GROUPS - 1))
    finish(second_pieces(GROUPS - 1))
    by_width(GROUPS - 1, lambda width: sent_turn(GROUPS - 1, 2, width))

    @pl.loop(0, near_codes.shape[0])
    def _(piece):
        for copy in far_copies(piece * half_rows):
            copy.wait_send()

    finish(last)

    for back in range(2):
        for which in range(3):
            tails[back, which] = coded[which, pl.ds(step_count - 1 - back, CHUNKS, stride=step_count), :]
    tail_copy = pltpu.make_async_remote_copy(
        src_ref=tails, dst_ref=sib_tails, send_sem=tail_send, recv_sem=tail_recv,
        device_id=sibling, device_id_type=MESH,
    )
    tail_copy.start()

    def spread(row):
        return jnp.broadcast_to(row, (CHUNKS, LANES))

    tap_rows = [[spread(taps[lag, which : which + 1, :]) for which in range(3)] for lag in range(3)]
    decay_rows = [spread(decays[mode : mode + 1, :]) for mode in range(modes)]
    index = lax.broadcasted_iota(jnp.int32, (CHUNKS, LANES), 0)
    odd = lax.rem(index, 2) == 1

    def before_chunk(back, which):
        own = pltpu.roll(tails[back, which], 1, 0)
        other = sib_tails[back, which]
        up = pltpu.roll(other, 1, 0)
        down = pltpu.roll(other, CHUNKS - 1, 0)
        outside = jnp.where(core == 0, jnp.where(index == 0, 0.0, up), down)
        return jnp.where(odd, own, outside)

    half_modes = modes // 2

    def load_step(step):
        return tuple(coded[which, pl.ds(step, CHUNKS, stride=step_count), :] for which in range(3))

    def featurize(step, now, newer, older):
        feat = [
            tap_rows[0][which] * now[which]
            + tap_rows[1][which] * newer[which]
            + tap_rows[2][which] * older[which]
            for which in range(3)
        ]
        drive = feat[1] * feat[2]
        at = pl.ds(pl.multiple_of(step * CHUNKS, CHUNKS), CHUNKS)
        queries[at, :] = feat[0]
        drives[at, :] = drive
        return drive

    def advance(states, drive, half):
        return tuple(
            decay_rows[half * half_modes + mode] * states[mode] + drive for mode in range(half_modes)
        )

    def first_pass(step, carry):
        older, newer, states = carry
        now = load_step(step)
        drive = featurize(step, now, newer, older)
        return newer, now, advance(states, drive, 0)

    def load_drive(step):
        return drives[pl.ds(pl.multiple_of(step * CHUNKS, CHUNKS), CHUNKS), :]

    def send_ends(half, states):
        for mode in range(half_modes):
            ends[half, mode * CHUNKS : (mode + 1) * CHUNKS, :] = states[mode]
        end_copy(half).start()

    def end_copy(half):
        return pltpu.make_async_remote_copy(
            src_ref=ends.at[half], dst_ref=sib_ends.at[half],
            send_sem=end_send.at[half], recv_sem=end_recv.at[half],
            device_id=sibling, device_id_type=MESH,
        )

    def start_states(half):
        end_copy(half).wait_recv()
        state = jnp.zeros((half_modes, LANES), F32)
        ratio = chunk_decays[half * half_modes : (half + 1) * half_modes, :]
        for run in range(CHUNKS // 2):
            for owner in range(2):
                for chunk in (2 * run, 2 * run + 1):
                    rows_at = pl.ds(chunk, half_modes, stride=CHUNKS)
                    starts[owner, rows_at, :] = state
                    ended = jnp.where(core == owner, ends[half, rows_at, :], sib_ends[half, rows_at, :])
                    state = ratio * state + ended
        return tuple(starts[core, mode * CHUNKS : (mode + 1) * CHUNKS, :] for mode in range(half_modes))

    zeros = tuple(jnp.zeros((CHUNKS, LANES), F32) for _ in range(half_modes))
    step_0, step_1 = load_step(0), load_step(1)
    _, _, states = lax.fori_loop(2, step_count, first_pass, (step_0, step_1, zeros), unroll=2)
    tail_copy.wait_recv()
    back_1 = tuple(before_chunk(0, which) for which in range(3))
    back_2 = tuple(before_chunk(1, which) for which in range(3))
    drive_0 = featurize(0, step_0, back_1, back_2)
    drive_1 = featurize(1, step_1, step_0, back_1)
    states = tuple(
        states[mode] + spread(fix_decays[mode : mode + 1, :]) * (decay_rows[mode] * drive_0 + drive_1)
        for mode in range(half_modes)
    )
    send_ends(0, states)
    states = lax.fori_loop(
        0, step_count, lambda step, held: advance(held, load_drive(step), 1), zeros, unroll=4
    )
    send_ends(1, states)
    coeff_rows = [spread(coeffs[mode : mode + 1, :]) for mode in range(modes)]
    skip_row = spread(skip)

    def weigh(states, half):
        parts = [coeff_rows[half * half_modes + mode] * states[mode] for mode in range(half_modes)]
        while len(parts) > 1:
            parts = [parts[i] + parts[i + 1] for i in range(0, len(parts), 2)]
        return parts[0]

    def middle_pass(step, states):
        at = pl.ds(pl.multiple_of(step * CHUNKS, CHUNKS), CHUNKS)
        drive = drives[at, :]
        states = advance(states, drive, 0)
        gated[at, :] = weigh(states, 0) + skip_row * drive
        return states

    lead = LEAD_BLOCKS * (step_count // 8)
    held_0 = lax.fori_loop(0, lead, middle_pass, start_states(0), unroll=4)

    out_rows = out_ref.shape[0]
    blocks = step_count // out_rows
    channel = pl.multiple_of((seq * 2 + high) * LANES, LANES)

    def second_pass(step, states):
        at = pl.ds(pl.multiple_of(step * CHUNKS, CHUNKS), CHUNKS)
        states = advance(states, drives[at, :], 1)
        gated[at, :] = queries[at, :] * (gated[at, :] + weigh(states, 1))
        return states

    place = out_ref.at[:, pl.ds(channel, LANES)]
    first_seat = core * 4

    def send_outs(block):
        row = first_seat + block // 4
        tp_at = lax.rem(block, 4)
        for chunk in range(CHUNKS):
            seq_at = row + (chunk // 2) * 8 + (chunk % 2) * 2
            is_me = jnp.logical_and(seq_at == seq, tp_at == tp)

            @pl.when(is_me)
            def _():
                pltpu.make_async_copy(staged.at[block, chunk], place, out_recv).start()

            @pl.when(jnp.logical_not(is_me))
            def _():
                pltpu.make_async_remote_copy(
                    src_ref=staged.at[block, chunk], dst_ref=place, send_sem=out_send, recv_sem=out_recv,
                    device_id=(seq_at, tp_at), device_id_type=MESH,
                ).start()

    def whole_pass(step, both):
        at = pl.ds(pl.multiple_of(step * CHUNKS, CHUNKS), CHUNKS)
        drive = drives[at, :]
        states_0, states_1 = advance(both[0], drive, 0), advance(both[1], drive, 1)
        total = (weigh(states_0, 0) + skip_row * drive) + weigh(states_1, 1)
        gated[at, :] = queries[at, :] * total
        return states_0, states_1

    def out_block(block, states, step_pass):
        states = lax.fori_loop(
            0, out_rows, lambda step, held: step_pass(block * out_rows + step, held), states, unroll=4
        )
        for chunk in range(CHUNKS):
            taken = gated[pl.ds(block * (out_rows * CHUNKS) + chunk, out_rows, stride=CHUNKS), :]
            staged[block, chunk] = taken.astype(BF16)
        send_outs(block)
        return states

    held_1 = lax.fori_loop(
        0, LEAD_BLOCKS, lambda block, held: out_block(block, held, second_pass), start_states(1)
    )
    lax.fori_loop(
        LEAD_BLOCKS, blocks, lambda block, held: out_block(block, held, whole_pass), (held_0, held_1)
    )

    tail_copy.wait_send()
    for half in range(2):
        end_copy(half).wait_send()
    pltpu.make_async_copy(out_ref, out_ref, out_recv).wait()
    sent = staged.at[pl.ds(1, blocks - 1)]
    pltpu.make_async_copy(sent, sent, out_send).wait()
    most = staged.at[0, pl.ds(1, CHUNKS - 1)]
    pltpu.make_async_copy(most, most, out_send).wait()

    @pl.when(core != layer)
    def _():
        pltpu.make_async_copy(staged.at[0, 0], staged.at[0, 0], out_send).wait()


def on_device(x_codes, w_codes, req_mult, req_shift, short_codes, residue_codes, rates, skip_gain):
    rows, feats = x_codes.shape
    seq_devs = lax.axis_size("seq")
    tp_devs = lax.axis_size("tp")
    cols = w_codes.shape[2]
    positions = rows * seq_devs // 2
    modes = residue_codes.shape[0]
    out_rows = rows // tp_devs
    steps = positions // CHUNKS
    blocks = steps // out_rows
    pieces = 2 * positions // rows
    w_rows = 256
    w_chunks = feats // w_rows
    small = (req_mult, req_shift, short_codes, residue_codes, rates, skip_gain.reshape(1, -1))
    dma = pltpu.SemaphoreType.DMA
    return pl.pallas_call(
        hyena_kernel,
        out_shape=pltpu.VMEM((out_rows, cols * seq_devs), BF16),
        in_specs=[pl.BlockSpec(memory_space=pl.ANY)] * 8,
        out_specs=pl.BlockSpec(memory_space=pltpu.VMEM),
        scratch_shapes=[
            *(pltpu.VMEM(array.shape, array.dtype) for array in small),
            dma((len(small),)),
            pltpu.VMEM((rows, feats), jnp.int32),
            pltpu.VMEM((rows, feats), BF16),
            pltpu.VMEM((seq_devs // 2, 2, rows, feats), BF16),
            pltpu.VMEM((w_chunks, 3, w_rows, cols), jnp.int32),
            pltpu.VMEM((2, feats, 3 * cols), BF16),
            pltpu.VMEM((positions, 3 * LANES), F32),
            pltpu.VMEM((pieces, rows // 2, 3 * LANES), jnp.int16),
            pltpu.VMEM((pieces, 1, 3 * LANES), F32),
            pltpu.VMEM((pieces, rows // 2, 3 * LANES), jnp.int16),
            pltpu.VMEM((pieces, 1, 3 * LANES), F32),
            pltpu.VMEM((3, positions, LANES), F32),
            pltpu.VMEM((2, 3, CHUNKS, LANES), F32),
            pltpu.VMEM((2, 3, CHUNKS, LANES), F32),
            pltpu.VMEM((2, modes // 2 * CHUNKS, LANES), F32),
            pltpu.VMEM((2, modes // 2 * CHUNKS, LANES), F32),
            pltpu.VMEM((2, modes // 2 * CHUNKS, LANES), F32),
            pltpu.VMEM((positions, LANES), F32),
            pltpu.VMEM((positions, LANES), F32),
            pltpu.VMEM((positions, LANES), F32),
            pltpu.VMEM((blocks, CHUNKS, out_rows, LANES), BF16),
            dma,
            dma((2, 2)),
            dma((2, 2)),
            dma((w_chunks,)),
            dma((w_chunks,)),
            dma((w_chunks,)),
            dma((2, 2, 3 * GROUPS)),
            dma((2, 2, 3 * GROUPS)),
            dma((2 * pieces,)),
            dma((2 * pieces,)),
            dma((pieces,)),
            dma((pieces,)),
            dma((pieces,)),
            dma((pieces,)),
            dma,
            dma,
            dma((2,)),
            dma((2,)),
            dma,
            dma,
        ],
        compiler_params=pltpu.CompilerParams(
            collective_id=0, has_side_effects=True, vmem_limit_bytes=56 * 1024 * 1024
        ),
    )(x_codes, w_codes, *small)


def solution(mesh):
    placed = (
        P("seq", "tp"),
        P(None, "tp", "seq"),
        P(None, "seq"),
        P(None, "seq"),
        P(None, None, "seq"),
        P(None, "seq"),
        P(None, "seq"),
        P("seq"),
    )
    return jax.shard_map(
        on_device, mesh=mesh, in_specs=placed, out_specs=P(("seq", "tp"), None), check_vma=False
    )
```

```python
import functools
import math

import jax
import jax.numpy as jnp
from jax import lax
from jax.experimental import pallas as pl
from jax.experimental.pallas import tpu as pltpu
from jax.sharding import PartitionSpec as P

MESH = pl.DeviceIdType.MESH
F32 = jnp.float32
BF16 = jnp.bfloat16
LANES = 128
CHUNKS = 8
RING = 4
GROUPS = 5
LATE = 512
WHOLE_FROM = 3
LEAD_BLOCKS = 4


def halves_of(which, array):
    return jnp.where(which == 0, array[..., :LANES], array[..., LANES:])


def small_expm1_neg(z):
    poly = jnp.ones_like(z)
    for order in range(8, 1, -1):
        poly = 1.0 - (z * (1.0 / order)) * poly
    return z * poly


def hyena_kernel(
    x_hbm, w_hbm, mult_hbm, shift_hbm, short_hbm, residue_hbm, rates_hbm, skip_hbm,
    out_ref,
    mult_ref, shift_ref, short_ref, residue_ref, rates_ref, skip_ref, small_sem,
    raw_x, own_x, all_x, raw_w, both_w, sums, near_codes, near_steps, far_codes, far_steps, coded, tails, sib_tails, ends, sib_ends,
    starts, queries, drives, gated, staged,
    x_sem, first_send, first_recv, raw_sem, w_send, w_recv, ring_send, ring_recv, late_send, late_recv,
    far_send, far_recv, step_send, step_recv, tail_send, tail_recv, end_send, end_recv, out_send, out_recv,
):
    seq = lax.axis_index("seq")
    tp = lax.axis_index("tp")
    y = lax.rem(seq, 4)
    layer = lax.rem(seq // 4, 2)
    x = seq // 8
    core = lax.rem(tp, 2)
    high = tp // 2
    rows, feats = own_x.shape
    half_rows = rows // 2
    early = feats - LATE
    modes = residue_ref.shape[0]
    step_count = coded.shape[1] // CHUNKS

    def device(x_at, y_at, layer_at, high_at, core_at):
        return ((x_at * 2 + layer_at) * 4 + y_at, high_at * 2 + core_at)

    def wrap(value):
        return lax.rem(value + 2 * RING, RING)

    barrier = pltpu.get_barrier_semaphore()
    column = layer * 2 + high * 4 + core

    def greet(target):
        pl.semaphore_signal(barrier, inc=1, device_id=target, device_id_type=MESH)

    for offset in range(1, 8):
        other = lax.rem(column + offset, 8)
        greet(device(x, y, lax.rem(other // 2, 2), other // 4, lax.rem(other, 2)))
    for step in (1, RING - 1):
        greet(device(wrap(x + step), y, layer, high, core))
        greet(device(x, wrap(y + step), layer, high, core))

    raw_copy = pltpu.make_async_copy(x_hbm, raw_x, x_sem)
    raw_copy.start()
    w_chunks = raw_w.shape[0]
    w_rows = raw_w.shape[2]
    for chunk in range(w_chunks):
        pltpu.make_async_copy(
            w_hbm.at[:, pl.ds(chunk * w_rows, w_rows), :], raw_w.at[chunk], raw_sem.at[chunk]
        ).start()

    small_copies = [
        pltpu.make_async_copy(source, target, small_sem.at[number])
        for number, (source, target) in enumerate(
            [
                (mult_hbm, mult_ref), (shift_hbm, shift_ref), (short_hbm, short_ref),
                (residue_hbm, residue_ref), (rates_hbm, rates_ref), (skip_hbm, skip_ref),
            ]
        )
    ]
    for copy in small_copies:
        copy.start()
    raw_copy.wait()
    own_x[...] = raw_x[...].astype(F32).astype(BF16)

    def convert_chunk(chunk):
        pltpu.make_async_copy(
            w_hbm.at[:, pl.ds(chunk * w_rows, w_rows), :], raw_w.at[chunk], raw_sem.at[chunk]
        ).wait()
        for which in range(3):
            for half in range(2):
                place = pl.multiple_of((half ^ high) * (3 * LANES) + which * LANES, LANES)
                both_w[core, pl.ds(pl.multiple_of(chunk * w_rows, w_rows), w_rows), pl.ds(place, LANES)] = (
                    raw_w[chunk, which, :, half * LANES : (half + 1) * LANES].astype(F32).astype(BF16)
                )

    pl.semaphore_wait(barrier, 11)

    home = x * 4 + y

    def by_width(group, action):
        whole = jnp.logical_or(core == layer, jnp.asarray(group >= WHOLE_FROM))

        @pl.when(whole)
        def _():
            action(feats)

        @pl.when(jnp.logical_not(whole))
        def _():
            action(early)

    def first_copy(part, across):
        at = pl.ds(part * half_rows, half_rows)
        lanes = pl.ds(0, early if across else feats)
        return pltpu.make_async_remote_copy(
            src_ref=own_x.at[at, lanes], dst_ref=all_x.at[home, core, at, lanes],
            send_sem=first_send.at[int(across), part], recv_sem=first_recv.at[core, part],
            device_id=device(x, y, 1 - layer if across else layer, high, layer), device_id_type=MESH,
        )

    for part in range(2):
        @pl.when(core == layer)
        def _():
            at = pl.ds(part * half_rows, half_rows)
            pltpu.make_async_copy(
                own_x.at[at, :], all_x.at[home, core, at, :], first_recv.at[core, part]
            ).start()

        @pl.when(core != layer)
        def _():
            first_copy(part, False).start()

        first_copy(part, True).start()

    sibling = device(x, y, layer, high, 1 - core)

    def w_copy(chunk):
        piece = both_w.at[core, pl.ds(pl.multiple_of(chunk * w_rows, w_rows), w_rows), :]
        return pltpu.make_async_remote_copy(
            src_ref=piece, dst_ref=piece, send_sem=w_send.at[chunk], recv_sem=w_recv.at[chunk],
            device_id=sibling, device_id_type=MESH,
        )

    def w_arrival(chunk):
        piece = both_w.at[1 - core, pl.ds(pl.multiple_of(chunk * w_rows, w_rows), w_rows), :]
        return pltpu.make_async_remote_copy(
            src_ref=piece, dst_ref=piece, send_sem=w_send.at[chunk], recv_sem=w_recv.at[chunk],
            device_id=sibling, device_id_type=MESH,
        )

    def piece_of(axis, group, along):
        shifted = jnp.maximum(group - 1, 0)
        first = jnp.where(group == 0, 1, 0)
        if axis == 0:
            return wrap(x + along) * 4 + wrap(y + shifted), 1 - first
        return wrap(x + shifted) * 4 + wrap(y + along), first

    def part_rows(part):
        return pl.ds(pl.multiple_of(part * half_rows, half_rows), half_rows)

    def ring_copy(axis, way, group, turn, along, feat, width):
        slot, part = piece_of(axis, group, along)
        unit = all_x.at[slot, feat, part_rows(part), pl.ds(0, width)]
        step = 1 if way == 0 else -1
        target = (
            device(wrap(x + step), y, layer, high, core)
            if axis == 0
            else device(x, wrap(y + step), layer, high, core)
        )
        return pltpu.make_async_remote_copy(
            src_ref=unit, dst_ref=unit,
            send_sem=ring_send.at[axis, way, group * 3 + turn],
            recv_sem=ring_recv.at[axis, way, group * 3 + turn],
            device_id=target, device_id_type=MESH,
        )

    def own_feat(turn):
        return core if turn == 0 else 1 - core

    def send_own(group, width, axes=(0, 1), turns=(0, 1)):
        for turn in turns:
            for axis in axes:
                for way in range(2):
                    ring_copy(axis, way, group, turn, 0, own_feat(turn), width).start()

    def send_on(group, width):
        for axis in range(2):
            for way in range(2):
                ring_copy(axis, way, group, 2, -1 if way == 0 else 1, way, width).start()

    def wait_own(group, width):
        for turn in range(2):
            for axis in range(2):
                for way in range(2):
                    ring_copy(axis, way, group, turn, -1 if way == 0 else 1, own_feat(turn), width).wait_recv()

    def wait_on(group, width):
        for axis in range(2):
            for way in range(2):
                ring_copy(axis, way, group, 2, 2, way, width).wait_recv()

    def late_copies(pieces):
        for slot, part in pieces:
            for feat in range(2):
                place = all_x.at[slot, feat, part_rows(part), pl.ds(early, LATE)]
                number = slot * 4 + part * 2 + feat
                yield pltpu.make_async_remote_copy(
                    src_ref=place, dst_ref=place,
                    send_sem=late_send.at[number], recv_sem=late_recv.at[number],
                    device_id=device(x, y, 1 - layer, high, core), device_id_type=MESH,
                )

    def send_late(pieces):
        @pl.when(core == layer)
        def _():
            for copy in late_copies(pieces):
                copy.start()

    def wait_late(pieces):
        @pl.when(core != layer)
        def _():
            for copy in late_copies(pieces):
                copy.wait_recv()

    far_home = device(x, y, layer, 1 - high, core)

    def far_copies(row):
        piece = row // half_rows
        return (
            pltpu.make_async_remote_copy(
                src_ref=near_codes.at[piece], dst_ref=far_codes.at[piece],
                send_sem=far_send.at[piece], recv_sem=far_recv.at[piece],
                device_id=far_home, device_id_type=MESH,
            ),
            pltpu.make_async_remote_copy(
                src_ref=near_steps.at[piece], dst_ref=far_steps.at[piece],
                send_sem=step_send.at[piece], recv_sem=step_recv.at[piece],
                device_id=far_home, device_id_type=MESH,
            ),
        )

    def product(pieces, first, stop):
        total = None
        for feat in range(2):
            left = jnp.concatenate(
                [all_x[slot, feat, part_rows(part), :] for slot, part in pieces], axis=0
            )
            term = jnp.dot(left, both_w[feat, :, first:stop], preferred_element_type=F32)
            total = term if total is None else total + term
        return [total[index * half_rows : (index + 1) * half_rows] for index in range(len(pieces))]

    def put_sums(pieces, parts, first):
        for (slot, part), values in zip(pieces, parts):
            row = pl.multiple_of(slot * rows + part * half_rows, half_rows)
            sums[pl.ds(row, half_rows), first : first + values.shape[1]] = values

    def put_codes(pieces, parts):
        for (slot, part), away in zip(pieces, parts):
            piece = slot * 2 + part
            peak = jnp.maximum(jnp.max(jnp.abs(away), axis=0, keepdims=True), 1.0)
            near_steps[piece] = peak * (1.0 / 32767.0)
            near_codes[piece] = jnp.round(away * (32767.0 / peak)).astype(jnp.int32).astype(jnp.int16)
        for slot, part in pieces:
            for copy in far_copies(slot * rows + part * half_rows):
                copy.start()

    def multiply(pieces):
        parts = product(pieces, 0, 6 * LANES)
        put_sums(pieces, [values[:, : 3 * LANES] for values in parts], 0)
        put_codes(pieces, [values[:, 3 * LANES :] for values in parts])

    def multiply_last(pieces):
        parts = product(pieces, 2 * LANES, 6 * LANES)
        put_codes(pieces, [values[:, LANES:] for values in parts])
        put_sums(pieces, [values[:, :LANES] for values in parts], 2 * LANES)
        put_sums(pieces, product(pieces, 0, 2 * LANES), 0)

    def finish(pieces):
        for slot, part in pieces:
            piece = slot * 2 + part
            for copy in far_copies(piece * half_rows):
                copy.wait_recv()
            at = pl.ds(pl.multiple_of(piece * half_rows, half_rows), half_rows)
            for which in range(3):
                lanes = slice(which * LANES, (which + 1) * LANES)
                away = far_codes[piece, :, lanes].astype(jnp.int32).astype(F32) * far_steps[piece, :, lanes]
                total = (sums[at, lanes] + away) * requant[which : which + 1, :]
                coded[which, at, :] = jnp.clip(total, -127.0, 127.0).astype(BF16).astype(F32)

    def near_pieces(group):
        return [piece_of(axis, group, along) for axis in range(2) for along in (-1, 1)]

    def next_pieces(group):
        return [piece_of(axis, group, 2) for axis in range(2)]

    def second_pieces(group):
        start = group == 0
        return [
            (jnp.where(start, home, slot), jnp.where(start, axis, part))
            for axis, (slot, part) in enumerate(next_pieces(jnp.maximum(group - 1, 0)))
        ]

    def begin_ring(width):
        for part in range(2):
            for turn in range(2):
                feat = own_feat(turn)
                landed = all_x.at[home, feat, pl.ds(part * half_rows, half_rows), pl.ds(0, width)]
                pltpu.make_async_copy(landed, landed, first_recv.at[feat, part]).wait()
                send_own(0, width, (part,), (turn,))
        send_own(1, width)

    @pl.when(core == layer)
    def _():
        for turn in range(2):
            feat = own_feat(turn)
            for part in range(2):
                landed = all_x.at[home, feat, pl.ds(part * half_rows, half_rows), :]
                pltpu.make_async_copy(landed, landed, first_recv.at[feat, part]).wait()
                send_own(0, feats, (part,), (turn,))
        send_own(1, feats)

    for copy in small_copies:
        copy.wait()
    requant = halves_of(high, mult_ref[...].astype(F32) * jnp.exp2(-shift_ref[...].astype(F32)))
    taps = halves_of(high, short_ref[...].astype(F32) * (1.0 / 8192.0))
    rates = halves_of(high, rates_ref[...])
    coeffs = (
        halves_of(high, residue_ref[...].astype(F32))
        * (1.0 / (127.0 * math.sqrt(modes)))
        * jnp.sqrt(small_expm1_neg(2.0 * rates))
    )
    skip = halves_of(high, skip_ref[...])
    decays = jnp.exp(-rates)
    fix_decays = jnp.exp(-rates * float(step_count - 2))
    chunk_decays = jnp.exp(-rates * float(step_count))

    @pl.loop(0, w_chunks)
    def _(chunk):
        convert_chunk(chunk)
        w_copy(chunk).start()

    @pl.when(core != layer)
    def _():
        begin_ring(early)

    @pl.loop(0, GROUPS)
    def _(group):
        def first_half(width):
            wait_own(group, width)
            send_on(group, width)

        by_width(group, first_half)
        near = near_pieces(group)

        @pl.when(group < WHOLE_FROM)
        def _():
            send_late(near)

        @pl.when(group == 0)
        def _():
            @pl.loop(0, w_chunks)
            def _(chunk):
                w_arrival(chunk).wait_recv()

        @pl.when(group < WHOLE_FROM)
        def _():
            wait_late(near)

        multiply(near)

        @pl.when(group > 0)
        def _():
            finish(near_pieces(group - 1))

        @pl.when(group > 0)
        def _():
            by_width(group - 1, lambda width: wait_on(group - 1, width))

        second = second_pieces(group)

        @pl.when(group <= WHOLE_FROM)
        def _():
            send_late(second)
            wait_late(second)

        @pl.when(group + 2 < GROUPS)
        def _():
            by_width(group + 2, lambda width: send_own(group + 2, width))

        multiply(second)

        @pl.when(group > 0)
        def _():
            finish(second_pieces(group - 1))

    for part in range(2):
        first_copy(part, True).wait_send()

        @pl.when(core != layer)
        def _():
            first_copy(part, False).wait_send()

    @pl.loop(0, w_chunks)
    def _(chunk):
        w_copy(chunk).wait_send()

    def sent_turn(group, turn, width):
        for axis in range(2):
            for way in range(2):
                ring_copy(axis, way, group, turn, 0, 0, width).wait_send()

    @pl.loop(0, GROUPS)
    def _(group):
        def sent_own(width):
            for turn in range(2):
                sent_turn(group, turn, width)

        by_width(group, sent_own)

    @pl.loop(0, GROUPS - 1)
    def _(group):
        by_width(group, lambda width: sent_turn(group, 2, width))

    @pl.when(core == layer)
    def _():
        for copy in late_copies([(home, 0), (home, 1)]):
            copy.wait_send()

        @pl.loop(0, WHOLE_FROM)
        def _(group):
            for copy in late_copies(near_pieces(group) + next_pieces(group)):
                copy.wait_send()

    by_width(GROUPS - 1, lambda width: wait_on(GROUPS - 1, width))
    last = next_pieces(GROUPS - 1)
    multiply_last(last)
    finish(near_pieces(GROUPS - 1))
    finish(second_pieces(GROUPS - 1))
    by_width(GROUPS - 1, lambda width: sent_turn(GROUPS - 1, 2, width))

    @pl.loop(0, near_codes.shape[0])
    def _(piece):
        for copy in far_copies(piece * half_rows):
            copy.wait_send()

    finish(last)

    for back in range(2):
        for which in range(3):
            tails[back, which] = coded[which, pl.ds(step_count - 1 - back, CHUNKS, stride=step_count), :]
    tail_copy = pltpu.make_async_remote_copy(
        src_ref=tails, dst_ref=sib_tails, send_sem=tail_send, recv_sem=tail_recv,
        device_id=sibling, device_id_type=MESH,
    )
    tail_copy.start()

    def spread(row):
        return jnp.broadcast_to(row, (CHUNKS, LANES))

    tap_rows = [[spread(taps[lag, which : which + 1, :]) for which in range(3)] for lag in range(3)]
    decay_rows = [spread(decays[mode : mode + 1, :]) for mode in range(modes)]
    index = lax.broadcasted_iota(jnp.int32, (CHUNKS, LANES), 0)
    odd = lax.rem(index, 2) == 1

    def before_chunk(back, which):
        own = pltpu.roll(tails[back, which], 1, 0)
        other = sib_tails[back, which]
        up = pltpu.roll(other, 1, 0)
        down = pltpu.roll(other, CHUNKS - 1, 0)
        outside = jnp.where(core == 0, jnp.where(index == 0, 0.0, up), down)
        return jnp.where(odd, own, outside)

    half_modes = modes // 2

    def load_step(step):
        return tuple(coded[which, pl.ds(step, CHUNKS, stride=step_count), :] for which in range(3))

    def featurize(step, now, newer, older):
        feat = [
            tap_rows[0][which] * now[which]
            + tap_rows[1][which] * newer[which]
            + tap_rows[2][which] * older[which]
            for which in range(3)
        ]
        drive = feat[1] * feat[2]
        at = pl.ds(pl.multiple_of(step * CHUNKS, CHUNKS), CHUNKS)
        queries[at, :] = feat[0]
        drives[at, :] = drive
        return drive

    def advance(states, drive, half):
        return tuple(
            decay_rows[half * half_modes + mode] * states[mode] + drive for mode in range(half_modes)
        )

    def first_pass(step, carry):
        older, newer, states = carry
        now = load_step(step)
        drive = featurize(step, now, newer, older)
        return newer, now, advance(states, drive, 0)

    def load_drive(step):
        return drives[pl.ds(pl.multiple_of(step * CHUNKS, CHUNKS), CHUNKS), :]

    def send_ends(half, states):
        for mode in range(half_modes):
            ends[half, mode * CHUNKS : (mode + 1) * CHUNKS, :] = states[mode]
        end_copy(half).start()

    def end_copy(half):
        return pltpu.make_async_remote_copy(
            src_ref=ends.at[half], dst_ref=sib_ends.at[half],
            send_sem=end_send.at[half], recv_sem=end_recv.at[half],
            device_id=sibling, device_id_type=MESH,
        )

    def start_states(half):
        end_copy(half).wait_recv()
        state = jnp.zeros((half_modes, LANES), F32)
        ratio = chunk_decays[half * half_modes : (half + 1) * half_modes, :]
        for run in range(CHUNKS // 2):
            for owner in range(2):
                for chunk in (2 * run, 2 * run + 1):
                    rows_at = pl.ds(chunk, half_modes, stride=CHUNKS)
                    starts[owner, rows_at, :] = state
                    ended = jnp.where(core == owner, ends[half, rows_at, :], sib_ends[half, rows_at, :])
                    state = ratio * state + ended
        return tuple(starts[core, mode * CHUNKS : (mode + 1) * CHUNKS, :] for mode in range(half_modes))

    zeros = tuple(jnp.zeros((CHUNKS, LANES), F32) for _ in range(half_modes))
    step_0, step_1 = load_step(0), load_step(1)
    _, _, states = lax.fori_loop(2, step_count, first_pass, (step_0, step_1, zeros), unroll=2)
    tail_copy.wait_recv()
    back_1 = tuple(before_chunk(0, which) for which in range(3))
    back_2 = tuple(before_chunk(1, which) for which in range(3))
    drive_0 = featurize(0, step_0, back_1, back_2)
    drive_1 = featurize(1, step_1, step_0, back_1)
    states = tuple(
        states[mode] + spread(fix_decays[mode : mode + 1, :]) * (decay_rows[mode] * drive_0 + drive_1)
        for mode in range(half_modes)
    )
    send_ends(0, states)
    states = lax.fori_loop(
        0, step_count, lambda step, held: advance(held, load_drive(step), 1), zeros, unroll=8
    )
    send_ends(1, states)
    coeff_rows = [spread(coeffs[mode : mode + 1, :]) for mode in range(modes)]
    skip_row = spread(skip)

    def weigh(states, half):
        parts = [coeff_rows[half * half_modes + mode] * states[mode] for mode in range(half_modes)]
        while len(parts) > 1:
            parts = [parts[i] + parts[i + 1] for i in range(0, len(parts), 2)]
        return parts[0]

    def middle_pass(step, states):
        at = pl.ds(pl.multiple_of(step * CHUNKS, CHUNKS), CHUNKS)
        drive = drives[at, :]
        states = advance(states, drive, 0)
        gated[at, :] = weigh(states, 0) + skip_row * drive
        return states

    lead = LEAD_BLOCKS * (step_count // 8)
    held_0 = lax.fori_loop(0, lead, middle_pass, start_states(0), unroll=8)

    out_rows = out_ref.shape[0]
    blocks = step_count // out_rows
    channel = pl.multiple_of((seq * 2 + high) * LANES, LANES)

    def second_pass(step, states):
        at = pl.ds(pl.multiple_of(step * CHUNKS, CHUNKS), CHUNKS)
        states = advance(states, drives[at, :], 1)
        gated[at, :] = queries[at, :] * (gated[at, :] + weigh(states, 1))
        return states

    place = out_ref.at[:, pl.ds(channel, LANES)]
    first_seat = core * 4

    def send_outs(block):
        row = first_seat + block // 4
        tp_at = lax.rem(block, 4)
        for chunk in range(CHUNKS):
            seq_at = row + (chunk // 2) * 8 + (chunk % 2) * 2
            is_me = jnp.logical_and(seq_at == seq, tp_at == tp)

            @pl.when(is_me)
            def _():
                pltpu.make_async_copy(staged.at[block, chunk], place, out_recv).start()

            @pl.when(jnp.logical_not(is_me))
            def _():
                pltpu.make_async_remote_copy(
                    src_ref=staged.at[block, chunk], dst_ref=place, send_sem=out_send, recv_sem=out_recv,
                    device_id=(seq_at, tp_at), device_id_type=MESH,
                ).start()

    def whole_pass(step, both):
        at = pl.ds(pl.multiple_of(step * CHUNKS, CHUNKS), CHUNKS)
        drive = drives[at, :]
        states_0, states_1 = advance(both[0], drive, 0), advance(both[1], drive, 1)
        total = (weigh(states_0, 0) + skip_row * drive) + weigh(states_1, 1)
        gated[at, :] = queries[at, :] * total
        return states_0, states_1

    def out_block(block, states, step_pass):
        states = lax.fori_loop(
            0, out_rows, lambda step, held: step_pass(block * out_rows + step, held), states, unroll=8
        )
        for chunk in range(CHUNKS):
            taken = gated[pl.ds(block * (out_rows * CHUNKS) + chunk, out_rows, stride=CHUNKS), :]
            staged[block, chunk] = taken.astype(BF16)
        send_outs(block)
        return states

    held_1 = lax.fori_loop(
        0, LEAD_BLOCKS, lambda block, held: out_block(block, held, second_pass), start_states(1)
    )
    lax.fori_loop(
        LEAD_BLOCKS, blocks, lambda block, held: out_block(block, held, whole_pass), (held_0, held_1)
    )

    tail_copy.wait_send()
    for half in range(2):
        end_copy(half).wait_send()
    pltpu.make_async_copy(out_ref, out_ref, out_recv).wait()
    sent = staged.at[pl.ds(1, blocks - 1)]
    pltpu.make_async_copy(sent, sent, out_send).wait()
    most = staged.at[0, pl.ds(1, CHUNKS - 1)]
    pltpu.make_async_copy(most, most, out_send).wait()

    @pl.when(core != layer)
    def _():
        pltpu.make_async_copy(staged.at[0, 0], staged.at[0, 0], out_send).wait()


def on_device(x_codes, w_codes, req_mult, req_shift, short_codes, residue_codes, rates, skip_gain):
    rows, feats = x_codes.shape
    seq_devs = lax.axis_size("seq")
    tp_devs = lax.axis_size("tp")
    cols = w_codes.shape[2]
    positions = rows * seq_devs // 2
    modes = residue_codes.shape[0]
    out_rows = rows // tp_devs
    steps = positions // CHUNKS
    blocks = steps // out_rows
    pieces = 2 * positions // rows
    w_rows = 256
    w_chunks = feats // w_rows
    small = (req_mult, req_shift, short_codes, residue_codes, rates, skip_gain.reshape(1, -1))
    dma = pltpu.SemaphoreType.DMA
    return pl.pallas_call(
        hyena_kernel,
        out_shape=pltpu.VMEM((out_rows, cols * seq_devs), BF16),
        in_specs=[pl.BlockSpec(memory_space=pl.ANY)] * 8,
        out_specs=pl.BlockSpec(memory_space=pltpu.VMEM),
        scratch_shapes=[
            *(pltpu.VMEM(array.shape, array.dtype) for array in small),
            dma((len(small),)),
            pltpu.VMEM((rows, feats), jnp.int32),
            pltpu.VMEM((rows, feats), BF16),
            pltpu.VMEM((seq_devs // 2, 2, rows, feats), BF16),
            pltpu.VMEM((w_chunks, 3, w_rows, cols), jnp.int32),
            pltpu.VMEM((2, feats, 3 * cols), BF16),
            pltpu.VMEM((positions, 3 * LANES), F32),
            pltpu.VMEM((pieces, rows // 2, 3 * LANES), jnp.int16),
            pltpu.VMEM((pieces, 1, 3 * LANES), F32),
            pltpu.VMEM((pieces, rows // 2, 3 * LANES), jnp.int16),
            pltpu.VMEM((pieces, 1, 3 * LANES), F32),
            pltpu.VMEM((3, positions, LANES), F32),
            pltpu.VMEM((2, 3, CHUNKS, LANES), F32),
            pltpu.VMEM((2, 3, CHUNKS, LANES), F32),
            pltpu.VMEM((2, modes // 2 * CHUNKS, LANES), F32),
            pltpu.VMEM((2, modes // 2 * CHUNKS, LANES), F32),
            pltpu.VMEM((2, modes // 2 * CHUNKS, LANES), F32),
            pltpu.VMEM((positions, LANES), F32),
            pltpu.VMEM((positions, LANES), F32),
            pltpu.VMEM((positions, LANES), F32),
            pltpu.VMEM((blocks, CHUNKS, out_rows, LANES), BF16),
            dma,
            dma((2, 2)),
            dma((2, 2)),
            dma((w_chunks,)),
            dma((w_chunks,)),
            dma((w_chunks,)),
            dma((2, 2, 3 * GROUPS)),
            dma((2, 2, 3 * GROUPS)),
            dma((2 * pieces,)),
            dma((2 * pieces,)),
            dma((pieces,)),
            dma((pieces,)),
            dma((pieces,)),
            dma((pieces,)),
            dma,
            dma,
            dma((2,)),
            dma((2,)),
            dma,
            dma,
        ],
        compiler_params=pltpu.CompilerParams(
            collective_id=0, has_side_effects=True, vmem_limit_bytes=56 * 1024 * 1024
        ),
    )(x_codes, w_codes, *small)


def solution(mesh):
    placed = (
        P("seq", "tp"),
        P(None, "tp", "seq"),
        P(None, "seq"),
        P(None, "seq"),
        P(None, None, "seq"),
        P(None, "seq"),
        P(None, "seq"),
        P("seq"),
    )
    return jax.shard_map(
        on_device, mesh=mesh, in_specs=placed, out_specs=P(("seq", "tp"), None), check_vma=False
    )
```
